32 devices in a mesh: tm: 4 (over z), gx: 4 (over y, x), gy: 2 (over core).
Axes of the slice: x: 2, y: 2, z: 4, core: 2. Of those that a mesh axis runs over, the one named last changes fastest.
Arguments:
- states: float32 [8, 256, 256], P('tm', 'gx', 'gy'), may hold values from 0.5 to 1.5
- bed: float32 [256, 256], P('gx', 'gy'), may hold values from -3 to 3
- background_state: float32 [256, 256], P('gx', 'gy'), may hold values from 0.5 to 1.5
- ice_mask: int32 [256, 256], P('gx', 'gy'), may hold values 0 or 1
- flow_rate: float32 [256, 256], P('gx', 'gy'), may hold values from 0.02 to 0.1
- obs_cell: int32 [8, 4, 2, 512], P('tm', 'gx', 'gy'), may hold values from 0 to 8191
- obs_value: float32 [8, 4, 2, 512], P('tm', 'gx', 'gy'), may hold values from 0.5 to 1.5
Outputs:
- states_out: float32 [8, 256, 256], P('tm', 'gx', 'gy')
- bed_out: float32 [256, 256], P('gx', 'gy')
The draws below stay inside these ranges and needn't reach their ends.
All inputs are finite; a program needn't handle non-finite values. No bound on the sum of `ice_mask` on one device may be relied on, other than what follows from the above.
Results may differ from the reference program's by a relative error of at most 0.0001.
Values sent between devices are 32-bit elements; how exact they have to be, the bound alone decides.
No kernel may reach another device: no remote copies, remote signals or barrier semaphores. Data moves between devices by JAX's collectives and lax.ppermute only.
A program may use at most 64 MiB of HBM per device.

```python
import math
import jax
import jax.numpy as jnp
from jax import lax

CX = 64
CY = 128
OBS = 512
STEPS = 4
OUTER = 2
SLICES = 8
NX = 256
NY = 256
N_GX = 4
N_GY = 2


def set_ends(entries, rng, low, top_value):
    longest = entries.shape.index(max(entries.shape))
    spots = []
    for shift in (0, 1):
        where = [jax.random.randint(jax.random.fold_in(rng, axis), (), 0, length) for axis, length in enumerate(entries.shape)]
        where[longest] = (where[longest] + shift) % entries.shape[longest]
        spots.append(tuple(where))
    return entries.at[spots[0]].set(low).at[spots[1]].set(top_value)


def steps_of(own_key, extent, cuts, least, top_value):
    gain, own = 1.0, jax.random.fold_in(own_key, 6)
    for dim, blocks in cuts:
        steps = jnp.exp(jax.random.uniform(jax.random.fold_in(own, dim), (blocks,), jnp.float32, least / len(cuts), top_value / len(cuts)))
        gain = gain * jnp.repeat(steps, extent[dim] // blocks).reshape([-1 if axis == dim else 1 for axis in range(len(extent))])
    return gain


def scatter_about(rng, extent, scale, limit, pieces=(), kind=jnp.bfloat16):
    loudness = steps_of(rng, extent, pieces, -0.22, 0.18) if pieces else 1.0
    drawn = jax.random.normal(rng, extent, jnp.float32) * scale * loudness
    return jnp.minimum(jnp.maximum(drawn, -limit), limit).astype(kind)


def setup_inputs(seed: int = 0) -> dict:
    seeds = jax.random.split(jax.random.key(seed), 8)
    states = jnp.clip(0.5 + 1.0 * jax.random.uniform(seeds[0], (SLICES, NX, NY), jnp.float32) ** steps_of(seeds[0], (SLICES, NX, NY), ((0, 4), (1, 4), (2, 2)), -0.2, 0.2), 0.5, 1.5)
    bed = scatter_about(seeds[1], (NX, NY), 0.5, 3.0, ((0, 4), (1, 2)), jnp.float32)
    background_state = jnp.clip(0.5 + 1.0 * jax.random.uniform(seeds[2], (NX, NY), jnp.float32) ** steps_of(seeds[2], (NX, NY), ((0, 4), (1, 2)), -0.2, 0.2), 0.5, 1.5)
    ice_mask = set_ends((jax.random.randint(seeds[3], (NX, NY), 0, 8) < 7).astype(jnp.int32), jax.random.fold_in(seeds[3], 1), 0, 1)
    flow_rate = jnp.clip(jnp.exp(math.log(0.1) - 1.609438 * jax.random.uniform(seeds[4], (NX, NY), jnp.float32) ** steps_of(seeds[4], (NX, NY), ((0, 4), (1, 2)), -0.2, 0.2)), 0.02, 0.1)
    obs_cell = set_ends(jax.random.randint(seeds[5], (SLICES, N_GX, N_GY, OBS), 0, CX * CY), jax.random.fold_in(seeds[5], 1), 0, (CX * CY) - 1).astype(jnp.int32)
    obs_value = jnp.clip(0.5 + 1.0 * jax.random.uniform(seeds[6], (SLICES, N_GX, N_GY, OBS), jnp.float32) ** steps_of(seeds[6], (SLICES, N_GX, N_GY, OBS), ((0, 4), (1, 4), (2, 2)), -0.2, 0.2), 0.5, 1.5)
    return dict(states=states, bed=bed, background_state=background_state, ice_mask=ice_mask, flow_rate=flow_rate, obs_cell=obs_cell, obs_value=obs_value)


bed_rate = 0.1
state_rate = 0.5

def advance(thick, ground, maskf, rate):
    surface = ground + thick
    open_x = maskf[1:, :] * maskf[:-1, :]
    coef_x = 0.5 * (rate[1:, :] + rate[:-1, :]) * open_x
    mean_x = 0.5 * (thick[1:, :] + thick[:-1, :])
    flux_x = coef_x * mean_x * mean_x * (surface[1:, :] - surface[:-1, :])
    open_y = maskf[:, 1:] * maskf[:, :-1]
    coef_y = 0.5 * (rate[:, 1:] + rate[:, :-1]) * open_y
    mean_y = 0.5 * (thick[:, 1:] + thick[:, :-1])
    flux_y = coef_y * mean_y * mean_y * (surface[:, 1:] - surface[:, :-1])
    change = flux_x[1:, 1:-1] - flux_x[:-1, 1:-1] + (flux_y[1:-1, 1:] - flux_y[1:-1, :-1])
    return thick[1:-1, 1:-1] + change

def model(thick, ground, maskf, rate):
    for step in range(STEPS):
        thick = advance(jnp.pad(thick, 1), jnp.pad(ground, 1), jnp.pad(maskf, 1), jnp.pad(rate, 1))
    return thick

def reference(states, bed, background_state, ice_mask, flow_rate, obs_cell, obs_value):
    maskf = ice_mask.astype(jnp.float32)
    rows_tile = NX // N_GX
    cols_tile = NY // N_GY
    tile_row = (jnp.arange(N_GX, dtype=jnp.int32) * rows_tile)[None, :, None, None]
    tile_col = (jnp.arange(N_GY, dtype=jnp.int32) * cols_tile)[None, None, :, None]
    rows = tile_row + obs_cell // cols_tile
    cols = tile_col + obs_cell % cols_tile
    cell_index = (rows * NY + cols).astype(jnp.int32).reshape(SLICES, -1)
    observed = obs_value.reshape(SLICES, -1)
    bed_prior = bed
    for outer in range(OUTER):
        ground = bed
        final = lax.map(lambda thick: model(thick, ground, maskf, flow_rate), states)
        previous = jnp.concatenate([background_state[None], final[:-1]], axis=0)
        misfit = states - previous
        following = jnp.concatenate([misfit[1:], jnp.zeros_like(misfit[:1])], axis=0)
        predicted = jnp.take_along_axis(final.reshape(SLICES, -1), cell_index, axis=1)
        residual = predicted - observed

        def spread(pair):
            values, index = pair
            return jnp.zeros((NX * NY,), jnp.float32).at[index].add(values)
        forcing = lax.map(spread, (residual, cell_index)).reshape(SLICES, NX, NY) - following

        def pull_one(pair):
            thick, weight = pair
            _, pull = jax.vjp(lambda first, second: model(first, second, maskf, flow_rate), thick, ground)
            return pull(weight)
        grad_states, grad_beds = lax.map(pull_one, (states, forcing))
        bed_grad = lax.optimization_barrier(jnp.sum(grad_beds, axis=0))
        bed = bed - bed_rate * (bed_grad + (bed - bed_prior))
        states = states - state_rate * (misfit + grad_states)
    return (states, bed)
```

```python
import functools

import jax
import jax.numpy as jnp
from jax import lax
from jax.experimental import pallas as pl
from jax.experimental.pallas import tpu as pltpu
from jax.sharding import PartitionSpec as P

STEPS = 4
OUTER = 2
HALO = 2 * STEPS * OUTER
LANES = 128

bed_rate = 0.1
state_rate = 0.5


def partner(index, shift, count):
    if count & (count - 1) == 0:
        return index ^ shift
    return (index + shift) % count


def source(index, shift, count):
    if count & (count - 1) == 0:
        return index ^ shift
    return (index + count - shift) % count


def exchange(value, axis, shift):
    count = lax.axis_size(axis)
    return lax.ppermute(value, axis, [(i, partner(i, shift, count)) for i in range(count)])


def neighbour_swaps(axis):
    count = lax.axis_size(axis)
    if count == 1:
        return []
    first = [(i, i ^ 1) for i in range(count)]
    if count == 2:
        return [first]
    second = []
    for i in range(1, count, 2):
        j = (i + 1) % count
        second += [(i, j), (j, i)]
    return [first, second]


def call(kernel, out_shape, operands, scratch=()):
    spec = pl.BlockSpec(memory_space=pltpu.VMEM)
    return pl.pallas_call(
        kernel,
        out_shape=out_shape,
        in_specs=[spec] * len(operands),
        out_specs=jax.tree.map(lambda _: spec, out_shape),
        scratch_shapes=list(scratch),
        name=kernel.func.__name__,
    )(*operands)


def lane_of(shape):
    return lax.broadcasted_iota(jnp.int32, shape, len(shape) - 1)


def maps_of(cells, values, rows, cols):
    row = cells // cols
    col = cells % cols
    n = cells.shape[-1]
    at_row = lax.broadcasted_iota(jnp.int32, (rows, n), 0) == row
    at_col = lax.broadcasted_iota(jnp.int32, (cols, n), 0) == col
    left = jnp.where(at_row, 1.0, 0.0).astype(jnp.bfloat16)
    part1 = values.astype(jnp.bfloat16).astype(jnp.float32)
    rest = values - part1
    part2 = rest.astype(jnp.bfloat16).astype(jnp.float32)
    part3 = rest - part2

    def gather(weight):
        right = jnp.where(at_col, weight, 0.0).astype(jnp.bfloat16)
        return lax.dot_general(left, right, (((1,), (1,)), ((), ())), preferred_element_type=jnp.float32)

    return gather(1.0), gather(part1) + (gather(part2) + gather(part3))


def pack_kernel(dims, *refs):
    slices, rows, cols, obs, group, sides, cut, width, lanes = dims
    states, bed, back, mask, rate, cells, values = refs[:7]
    near = refs[7 : 7 + sides]
    blocks = refs[7 + sides : 7 + sides + group]
    statics = refs[7 + sides + group]
    me = lax.axis_index("tm")
    y = lax.axis_index("gy")
    last_y = lax.axis_size("gy") - 1
    lane = lane_of((rows, LANES))
    wide = lane_of((rows, lanes))
    even = (y & 1) == 0

    def beyond(get):
        if sides == 0:
            return jnp.zeros((rows, cols), jnp.float32)
        if sides == 1:
            return get(near[0])
        one, two = get(near[0]), get(near[1])
        return jnp.where((lane < cols // 2) == even, one, two)

    def cut_out(inside, outside, start, offset):
        shift = (offset - start + 4 * LANES) % LANES
        column = lane - offset + start
        picked = jnp.where(
            (column >= 0) & (column < cols),
            pltpu.roll(inside, shift, 1),
            pltpu.roll(outside, shift, 1),
        )
        return picked

    def packed(parts, start):
        out = jnp.zeros((rows, lanes), jnp.float32)
        for s, (inside, outside) in enumerate(parts):
            offset = s * width
            base = offset // LANES * LANES
            piece = cut_out(inside, outside, start, offset - base)
            if lanes != LANES:
                piece = jnp.concatenate([piece] * (lanes // LANES), axis=1)
            out = jnp.where((wide >= offset) & (wide < offset + width), piece, out)
        return out

    kinds = [[], [], []]
    for s in range(slices):
        kinds[0].append((states[s], beyond(lambda r: r[s * rows : (s + 1) * rows])))
        own = maps_of(cells[s : s + 1], values[s : s + 1], rows, cols)
        top = (slices + 4) * rows
        out = []
        for r in near:
            listed = r[top + 2 * s * (obs // LANES) : top + 2 * (s + 1) * (obs // LANES)]
            listed = [
                jnp.concatenate([listed[i * (obs // LANES) + j : i * (obs // LANES) + j + 1] for j in range(obs // LANES)], axis=1)
                for i in (0, 1)
            ]
            out.append(maps_of(listed[0].astype(jnp.int32), listed[1], rows, cols))
        for i in (0, 1):
            if sides == 0:
                outside = jnp.zeros((rows, cols), jnp.float32)
            elif sides == 1:
                outside = out[0][i]
            else:
                outside = jnp.where((lane < cols // 2) == even, out[0][i], out[1][i])
            kinds[1 + i].append((own[i], outside))
    for k in range(group):
        start = partner(me, k, group) * cut - HALO
        for i in range(3):
            blocks[k][i] = packed(kinds[i], start)
    start = me * cut - HALO
    for i, ref in enumerate((bed, back, mask, rate)):
        inside = ref[...]
        outside = beyond(lambda r: r[(slices + i) * rows : (slices + i + 1) * rows])
        if i == 2:
            outside = jnp.where((lane < cols // 2) & (y == last_y), 0.0, outside)
            outside = jnp.where((lane >= cols // 2) & (y == 0), 0.0, outside)
            inside = inside.astype(jnp.float32)
        statics[i] = packed([(inside, outside)] * slices, start)


def edge_kernel(dims, *refs):
    group, rows = dims
    blocks, statics, sends = refs[:group], refs[group], refs[group + 1 :]
    even = (lax.axis_index("gx") & 1) == 0
    for i, send in enumerate(sends):
        lower = even if i == 0 else jnp.logical_not(even)
        start = pl.multiple_of(jnp.where(lower, rows - HALO, 0), 8)
        for k in range(group):
            send[3 * k : 3 * k + 3] = blocks[k][:, pl.ds(start, HALO), :]
        send[3 * group : 3 * group + 4] = statics[:, pl.ds(start, HALO), :]


def main_kernel(dims, *refs):
    slices, rows, group, sides, cut, width, lanes = dims
    blocks, statics = refs[:group], refs[group]
    edges = refs[group + 1 : group + 1 + sides]
    outs = refs[group + 1 + sides : 2 * group + 1 + sides]
    state, count, total, fixed, final, misfit, keep, acc, coef = refs[2 * group + 1 + sides :]
    me = lax.axis_index("tm")
    x = lax.axis_index("gx")
    last_x = lax.axis_size("gx") - 1
    even = (x & 1) == 0
    full = rows + 2 * HALO

    def put(target, main, pieces):
        target[HALO : HALO + rows] = main
        if sides < 2:
            target[0:HALO] = jnp.zeros((HALO, lanes), jnp.float32)
            target[HALO + rows : full] = jnp.zeros((HALO, lanes), jnp.float32)
        for i, piece in enumerate(pieces):
            after = even if i == 0 else jnp.logical_not(even)
            target[pl.ds(pl.multiple_of(jnp.where(after, HALO + rows, 0), 8), HALO)] = piece

    for k in range(group):
        pair = source(me, k, group)
        for i, target in enumerate((state, count, total)):
            put(target.at[pair], blocks[k][i], [e[3 * k + i] for e in edges])
    for i in range(4):
        put(fixed.at[i], statics[i], [e[3 * group + i] for e in edges])

    row = lax.broadcasted_iota(jnp.int32, (full, lanes), 0)
    lane = lane_of((full, lanes))
    outside = ((row < HALO) & (x == 0)) | ((row >= HALO + rows) & (x == last_x))
    mask = jnp.where(outside, 0.0, fixed[2])
    rate = fixed[3]
    down = lambda v: pltpu.roll(v, v.shape[0] - 1, 0)
    up = lambda v: pltpu.roll(v, 1, 0)
    right = lambda v: pltpu.roll(v, lanes - 1, 1)
    left = lambda v: pltpu.roll(v, 1, 1)
    face_x = 0.25 * (rate + down(rate)) * (mask * down(mask))
    face_y = 0.25 * (rate + right(rate)) * (mask * right(mask))
    seam = lane % width == width - 1
    if lanes != slices * width:
        seam = seam | (lane >= slices * width)
    coef[0] = face_x
    coef[1] = jnp.where(seam, 0.0, face_y)
    prior = fixed[0]

    for outer in range(OUTER):
        low = 2 * STEPS * outer
        high = full - low
        size = high - low
        span = pl.ds(low, size)
        bed = fixed[0, span]
        coef[0, span] = jnp.where(row[:size] == size - 1, 0.0, coef[0, span])
        coef[2, span] = down(bed) - bed
        coef[3, span] = right(bed) - bed

        def forward(p, _):
            thick = state[p, span]
            for step in range(STEPS):
                after = thick
                for d, (ahead, behind) in enumerate(((down, up), (right, left))):
                    there = ahead(thick)
                    both = thick + there
                    slope = (there - thick) + coef[2 + d, span]
                    scaled = coef[d, span] * both
                    half = 0.5 * both
                    by_mean = scaled * slope
                    keep[p, step, 2 * d, span] = half * scaled
                    keep[p, step, 2 * d + 1, span] = by_mean
                    flux = half * by_mean
                    after = after + (flux - behind(flux))
                thick = after
            final[p, span] = thick
            return 0

        lax.fori_loop(0, group, forward, 0)
        here = lane[:size]

        def differ(p, _):
            own = final[p, span]
            before = final[jnp.maximum(p - 1, 0), span]
            start = jnp.where(p == 0, fixed[1, span], pltpu.roll(before, (lanes - (slices - 1) * width) % lanes, 1))
            earlier = jnp.where(here < width, start, pltpu.roll(own, width, 1))
            misfit[p, span] = state[p, span] - earlier
            return 0

        lax.fori_loop(0, group, differ, 0)
        acc[...] = jnp.zeros_like(acc)

        def backward(p, _):
            own = misfit[p, span]
            after = misfit[jnp.minimum(p + 1, group - 1), span]
            after = jnp.where(p == group - 1, 0.0, pltpu.roll(after, (slices - 1) * width, 1))
            later = jnp.where(here < (slices - 1) * width, pltpu.roll(own, lanes - width, 1), after)
            pull = count[p, span] * final[p, span] - total[p, span] - later
            for step in reversed(range(STEPS)):
                new = pull
                for d, (ahead, behind) in enumerate(((down, up), (right, left))):
                    jump = pull - ahead(pull)
                    by_slope = keep[p, step, 2 * d, span] * jump
                    by_mean = keep[p, step, 2 * d + 1, span] * jump
                    acc[d, span] = acc[d, span] + by_slope
                    new = new + ((by_mean - by_slope) + behind(by_mean + by_slope))
                pull = new
            state[p, span] = state[p, span] - state_rate * (own + pull)
            return 0

        lax.fori_loop(0, group, backward, 0)
        by_x, by_y = acc[0, span], acc[1, span]
        each = (up(by_x) - by_x) + (left(by_y) - by_y)
        summed = each
        for s in range(1, slices):
            summed = summed + pltpu.roll(each, lanes - s * width, 1)
        grad = summed
        for s in range(1, slices):
            grad = jnp.where(here >= s * width, pltpu.roll(summed, s * width, 1), grad)
        fixed[0, span] = bed - bed_rate * (grad + (bed - prior[low:high]))

    inner = slice(HALO, HALO + rows)
    place = lane_of((rows, LANES))

    def one_tile(value, come, go):
        if lanes != LANES:
            base = come // LANES * LANES
            value = jnp.concatenate([value, value[:, :LANES]], axis=1)
            low = pltpu.roll(value[:, base : base + LANES], (go - come) % LANES, 1)
            high = pltpu.roll(value[:, base + LANES : base + 2 * LANES], (go - come) % LANES, 1)
            return jnp.where(place - go + come - base < LANES, low, high)
        return pltpu.roll(value, (go - come) % LANES, 1)

    ground = one_tile(fixed[0, inner], HALO, slices * cut)
    for k in range(group):
        mine = state[partner(me, k, group), inner]
        out = ground
        for s in range(slices):
            piece = one_tile(mine, s * width + HALO, s * cut)
            out = jnp.where((place >= s * cut) & (place < (s + 1) * cut), piece, out)
        outs[k][...] = out


def join_kernel(dims, *refs):
    slices, rows, group, cut = dims
    pieces, states, bed = refs[:group], refs[group], refs[group + 1]
    me = lax.axis_index("tm")
    lane = lane_of((rows, LANES))
    outs = [jnp.zeros((rows, LANES), jnp.float32)] * (slices + 1)
    for k in range(group):
        block = source(me, k, group)
        here = (lane >= block * cut) & (lane < (block + 1) * cut)
        value = pieces[k][...]
        for s in range(slices + 1):
            shift = (block * cut - s * cut + LANES) % LANES
            outs[s] = jnp.where(here, pltpu.roll(value, shift, 1), outs[s])
    for s in range(slices):
        states[s] = outs[s]
    bed[...] = outs[slices]


def per_device(states, bed, background_state, ice_mask, flow_rate, obs_cell, obs_value):
    slices, rows, cols = states.shape
    obs = obs_cell.shape[-1]
    group = lax.axis_size("tm")
    cut = cols // group
    width = cut + 2 * HALO
    lanes = -(-slices * width // LANES) * LANES
    full = rows + 2 * HALO
    f32 = lambda *shape: jax.ShapeDtypeStruct(shape, jnp.float32)
    vmem = lambda *shape: pltpu.VMEM(shape, jnp.float32)

    cells = obs_cell.reshape(slices, obs)
    values = obs_value.reshape(slices, obs)
    listed = jnp.stack([cells.astype(jnp.float32), values], axis=1)
    raw = jnp.concatenate(
        [
            states.reshape(slices * rows, cols),
            bed,
            background_state,
            ice_mask.astype(jnp.float32),
            flow_rate,
            listed.reshape(-1, LANES),
        ],
        axis=0,
    )
    near = [lax.ppermute(raw, "gy", pairs) for pairs in neighbour_swaps("gy")]
    dims = (slices, rows, cols, obs, group, len(near), cut, width, lanes)
    *blocks, statics = call(
        functools.partial(pack_kernel, dims),
        [f32(3, rows, lanes)] * group + [f32(4, rows, lanes)],
        [states, bed, background_state, ice_mask, flow_rate, cells, values, *near],
    )
    blocks = [blocks[0]] + [exchange(blocks[k], "tm", k) for k in range(1, group)]
    swaps = neighbour_swaps("gx")
    edges = []
    if swaps:
        sends = call(
            functools.partial(edge_kernel, (group, rows)),
            [f32(3 * group + 4, HALO, lanes)] * len(swaps),
            [*blocks, statics],
        )
        edges = [lax.ppermute(send, "gx", pairs) for send, pairs in zip(sends, swaps)]
    packed = call(
        functools.partial(main_kernel, (slices, rows, group, len(edges), cut, width, lanes)),
        [f32(rows, LANES)] * group,
        [*blocks, statics, *edges],
        [vmem(group, full, lanes)] * 3
        + [vmem(4, full, lanes)]
        + [vmem(group, full, lanes)] * 2
        + [vmem(group, STEPS, 4, full, lanes), vmem(2, full, lanes), vmem(4, full, lanes)],
    )
    pieces = [packed[0]] + [exchange(packed[k], "tm", k) for k in range(1, group)]
    return tuple(
        call(
            functools.partial(join_kernel, (slices, rows, group, cut)),
            [f32(slices, rows, cols), f32(rows, cols)],
            pieces,
        )
    )


def solution(mesh):
    placed = (
        P("tm", "gx", "gy"),
        P("gx", "gy"),
        P("gx", "gy"),
        P("gx", "gy"),
        P("gx", "gy"),
        P("tm", "gx", "gy", None),
        P("tm", "gx", "gy", None),
    )
    return jax.shard_map(
        per_device,
        mesh=mesh,
        in_specs=placed,
        out_specs=(P("tm", "gx", "gy"), P("gx", "gy")),
        check_vma=False,
    )
```

```python
import functools

import jax
import jax.numpy as jnp
from jax import lax
from jax.experimental import pallas as pl
from jax.experimental.pallas import tpu as pltpu
from jax.sharding import PartitionSpec as P

STEPS = 4
OUTER = 2
HALO = 2 * STEPS * OUTER
LANES = 128

bed_rate = 0.1
state_rate = 0.5


def partner(index, shift, count):
    if count & (count - 1) == 0:
        return index ^ shift
    return (index + shift) % count


def source(index, shift, count):
    if count & (count - 1) == 0:
        return index ^ shift
    return (index + count - shift) % count


def exchange(value, axis, shift):
    count = lax.axis_size(axis)
    return lax.ppermute(value, axis, [(i, partner(i, shift, count)) for i in range(count)])


def neighbour_swaps(axis):
    count = lax.axis_size(axis)
    if count == 1:
        return []
    first = [(i, i ^ 1) for i in range(count)]
    if count == 2:
        return [first]
    second = []
    for i in range(1, count, 2):
        j = (i + 1) % count
        second += [(i, j), (j, i)]
    return [first, second]


def call(kernel, out_shape, operands, scratch=()):
    spec = pl.BlockSpec(memory_space=pltpu.VMEM)
    return pl.pallas_call(
        kernel,
        out_shape=out_shape,
        in_specs=[spec] * len(operands),
        out_specs=jax.tree.map(lambda _: spec, out_shape),
        scratch_shapes=list(scratch),
        name=kernel.func.__name__,
        compiler_params=pltpu.CompilerParams(vmem_limit_bytes=16 << 20),
    )(*operands)


def lane_of(shape):
    return lax.broadcasted_iota(jnp.int32, shape, len(shape) - 1)


def maps_of(cells, values, rows, cols):
    row = cells // cols
    col = cells % cols
    n = cells.shape[-1]
    at_row = lax.broadcasted_iota(jnp.int32, (rows, n), 0) == row
    at_col = lax.broadcasted_iota(jnp.int32, (cols, n), 0) == col
    left = jnp.where(at_row, 1.0, 0.0).astype(jnp.bfloat16)
    part1 = values.astype(jnp.bfloat16).astype(jnp.float32)
    rest = values - part1
    part2 = rest.astype(jnp.bfloat16).astype(jnp.float32)
    part3 = rest - part2

    def gather(weight):
        right = jnp.where(at_col, weight, 0.0).astype(jnp.bfloat16)
        return lax.dot_general(left, right, (((1,), (1,)), ((), ())), preferred_element_type=jnp.float32)

    return gather(1.0), gather(part1) + (gather(part2) + gather(part3))


def pack_kernel(dims, *refs):
    slices, rows, cols, obs, group, sides, cut, width, lanes = dims
    states, bed, back, mask, rate, cells, values = refs[:7]
    near = refs[7 : 7 + sides]
    blocks = refs[7 + sides : 7 + sides + group]
    statics = refs[7 + sides + group]
    me = lax.axis_index("tm")
    y = lax.axis_index("gy")
    last_y = lax.axis_size("gy") - 1
    lane = lane_of((rows, LANES))
    wide = lane_of((rows, lanes))
    even = (y & 1) == 0

    def beyond(get):
        if sides == 0:
            return jnp.zeros((rows, cols), jnp.float32)
        if sides == 1:
            return get(near[0])
        one, two = get(near[0]), get(near[1])
        return jnp.where((lane < cols // 2) == even, one, two)

    def cut_out(inside, outside, start, offset):
        shift = (offset - start + 4 * LANES) % LANES
        column = lane - offset + start
        picked = jnp.where(
            (column >= 0) & (column < cols),
            pltpu.roll(inside, shift, 1),
            pltpu.roll(outside, shift, 1),
        )
        return picked

    def packed(parts, start):
        out = jnp.zeros((rows, lanes), jnp.float32)
        for s, (inside, outside) in enumerate(parts):
            offset = s * width
            base = offset // LANES * LANES
            piece = cut_out(inside, outside, start, offset - base)
            if lanes != LANES:
                piece = jnp.concatenate([piece] * (lanes // LANES), axis=1)
            out = jnp.where((wide >= offset) & (wide < offset + width), piece, out)
        return out

    kinds = [[], [], []]
    for s in range(slices):
        kinds[0].append((states[s], beyond(lambda r: r[s * rows : (s + 1) * rows])))
        own = maps_of(cells[s : s + 1], values[s : s + 1], rows, cols)
        top = (slices + 4) * rows
        out = []
        for r in near:
            listed = r[top + 2 * s * (obs // LANES) : top + 2 * (s + 1) * (obs // LANES)]
            listed = [
                jnp.concatenate([listed[i * (obs // LANES) + j : i * (obs // LANES) + j + 1] for j in range(obs // LANES)], axis=1)
                for i in (0, 1)
            ]
            out.append(maps_of(listed[0].astype(jnp.int32), listed[1], rows, cols))
        for i in (0, 1):
            if sides == 0:
                outside = jnp.zeros((rows, cols), jnp.float32)
            elif sides == 1:
                outside = out[0][i]
            else:
                outside = jnp.where((lane < cols // 2) == even, out[0][i], out[1][i])
            kinds[1 + i].append((own[i], outside))
    for k in range(group):
        start = partner(me, k, group) * cut - HALO
        for i in range(3):
            blocks[k][i] = packed(kinds[i], start)
    start = me * cut - HALO
    for i, ref in enumerate((bed, back, mask, rate)):
        inside = ref[...]
        outside = beyond(lambda r: r[(slices + i) * rows : (slices + i + 1) * rows])
        if i == 2:
            outside = jnp.where((lane < cols // 2) & (y == last_y), 0.0, outside)
            outside = jnp.where((lane >= cols // 2) & (y == 0), 0.0, outside)
            inside = inside.astype(jnp.float32)
        statics[i] = packed([(inside, outside)] * slices, start)


def edge_kernel(dims, *refs):
    group, rows = dims
    blocks, statics, sends = refs[:group], refs[group], refs[group + 1 :]
    even = (lax.axis_index("gx") & 1) == 0
    for i, send in enumerate(sends):
        lower = even if i == 0 else jnp.logical_not(even)
        start = pl.multiple_of(jnp.where(lower, rows - HALO, 0), 8)
        for k in range(group):
            send[3 * k : 3 * k + 3] = blocks[k][:, pl.ds(start, HALO), :]
        send[3 * group : 3 * group + 4] = statics[:, pl.ds(start, HALO), :]


def main_kernel(dims, *refs):
    slices, rows, group, sides, cut, width, lanes = dims
    blocks, statics = refs[:group], refs[group]
    edges = refs[group + 1 : group + 1 + sides]
    outs = refs[group + 1 + sides : 2 * group + 1 + sides]
    state, count, total, fixed, final, misfit, keep, acc, coef = refs[2 * group + 1 + sides :]
    me = lax.axis_index("tm")
    x = lax.axis_index("gx")
    last_x = lax.axis_size("gx") - 1
    even = (x & 1) == 0
    full = rows + 2 * HALO

    def put(target, main, pieces):
        target[HALO : HALO + rows] = main
        if sides < 2:
            target[0:HALO] = jnp.zeros((HALO, lanes), jnp.float32)
            target[HALO + rows : full] = jnp.zeros((HALO, lanes), jnp.float32)
        for i, piece in enumerate(pieces):
            after = even if i == 0 else jnp.logical_not(even)
            target[pl.ds(pl.multiple_of(jnp.where(after, HALO + rows, 0), 8), HALO)] = piece

    for k in range(group):
        pair = source(me, k, group)
        for i, target in enumerate((state, count, total)):
            put(target.at[pair], blocks[k][i], [e[3 * k + i] for e in edges])
    for i in range(4):
        put(fixed.at[i], statics[i], [e[3 * group + i] for e in edges])

    row = lax.broadcasted_iota(jnp.int32, (full, lanes), 0)
    lane = lane_of((full, lanes))
    outside = ((row < HALO) & (x == 0)) | ((row >= HALO + rows) & (x == last_x))
    mask = jnp.where(outside, 0.0, fixed[2])
    rate = fixed[3]
    down = lambda v: pltpu.roll(v, v.shape[0] - 1, 0)
    up = lambda v: pltpu.roll(v, 1, 0)
    right = lambda v: pltpu.roll(v, lanes - 1, 1)
    left = lambda v: pltpu.roll(v, 1, 1)
    face_x = 0.25 * (rate + down(rate)) * (mask * down(mask))
    face_y = 0.25 * (rate + right(rate)) * (mask * right(mask))
    seam = lane % width == width - 1
    if lanes != slices * width:
        seam = seam | (lane >= slices * width)
    coef[0] = face_x
    coef[1] = jnp.where(seam, 0.0, face_y)
    prior = fixed[0]

    for outer in range(OUTER):
        low = 2 * STEPS * outer
        high = full - low
        size = high - low
        span = pl.ds(low, size)
        bed = fixed[0, span]
        coef[0, span] = jnp.where(row[:size] == size - 1, 0.0, coef[0, span])
        coef[2, span] = down(bed) - bed
        coef[3, span] = right(bed) - bed

        def forward(p, _):
            thick = state[p, span]
            for step in range(STEPS):
                after = thick
                for d, (ahead, behind) in enumerate(((down, up), (right, left))):
                    there = ahead(thick)
                    both = thick + there
                    slope = (there - thick) + coef[2 + d, span]
                    scaled = coef[d, span] * both
                    half = 0.5 * both
                    by_mean = scaled * slope
                    keep[p, step, 2 * d, span] = half * scaled
                    keep[p, step, 2 * d + 1, span] = by_mean
                    flux = half * by_mean
                    after = after + (flux - behind(flux))
                thick = after
            final[p, span] = thick
            return 0

        lax.fori_loop(0, group, forward, 0)
        here = lane[:size]

        def differ(p, _):
            own = final[p, span]
            before = final[jnp.maximum(p - 1, 0), span]
            start = jnp.where(p == 0, fixed[1, span], pltpu.roll(before, (lanes - (slices - 1) * width) % lanes, 1))
            earlier = jnp.where(here < width, start, pltpu.roll(own, width, 1))
            misfit[p, span] = state[p, span] - earlier
            return 0

        lax.fori_loop(0, group, differ, 0)
        acc[...] = jnp.zeros_like(acc)

        def backward(p, _):
            own = misfit[p, span]
            after = misfit[jnp.minimum(p + 1, group - 1), span]
            after = jnp.where(p == group - 1, 0.0, pltpu.roll(after, (slices - 1) * width, 1))
            later = jnp.where(here < (slices - 1) * width, pltpu.roll(own, lanes - width, 1), after)
            pull = count[p, span] * final[p, span] - total[p, span] - later
            for step in reversed(range(STEPS)):
                new = pull
                for d, (ahead, behind) in enumerate(((down, up), (right, left))):
                    jump = pull - ahead(pull)
                    by_slope = keep[p, step, 2 * d, span] * jump
                    by_mean = keep[p, step, 2 * d + 1, span] * jump
                    acc[d, span] = acc[d, span] + by_slope
                    new = new + ((by_mean - by_slope) + behind(by_mean + by_slope))
                pull = new
            state[p, span] = state[p, span] - state_rate * (own + pull)
            return 0

        lax.fori_loop(0, group, backward, 0)
        by_x, by_y = acc[0, span], acc[1, span]
        each = (up(by_x) - by_x) + (left(by_y) - by_y)
        summed = each
        for s in range(1, slices):
            summed = summed + pltpu.roll(each, lanes - s * width, 1)
        grad = summed
        for s in range(1, slices):
            grad = jnp.where(here >= s * width, pltpu.roll(summed, s * width, 1), grad)
        fixed[0, span] = bed - bed_rate * (grad + (bed - prior[low:high]))

    inner = slice(HALO, HALO + rows)
    place = lane_of((rows, LANES))

    def one_tile(value, come, go):
        if lanes != LANES:
            base = come // LANES * LANES
            value = jnp.concatenate([value, value[:, :LANES]], axis=1)
            low = pltpu.roll(value[:, base : base + LANES], (go - come) % LANES, 1)
            high = pltpu.roll(value[:, base + LANES : base + 2 * LANES], (go - come) % LANES, 1)
            return jnp.where(place - go + come - base < LANES, low, high)
        return pltpu.roll(value, (go - come) % LANES, 1)

    ground = one_tile(fixed[0, inner], HALO, slices * cut)
    for k in range(group):
        mine = state[partner(me, k, group), inner]
        out = ground
        for s in range(slices):
            piece = one_tile(mine, s * width + HALO, s * cut)
            out = jnp.where((place >= s * cut) & (place < (s + 1) * cut), piece, out)
        outs[k][...] = out


def join_kernel(dims, *refs):
    slices, rows, group, cut = dims
    pieces, states, bed = refs[:group], refs[group], refs[group + 1]
    me = lax.axis_index("tm")
    lane = lane_of((rows, LANES))
    outs = [jnp.zeros((rows, LANES), jnp.float32)] * (slices + 1)
    for k in range(group):
        block = source(me, k, group)
        here = (lane >= block * cut) & (lane < (block + 1) * cut)
        value = pieces[k][...]
        for s in range(slices + 1):
            shift = (block * cut - s * cut + LANES) % LANES
            outs[s] = jnp.where(here, pltpu.roll(value, shift, 1), outs[s])
    for s in range(slices):
        states[s] = outs[s]
    bed[...] = outs[slices]


def per_device(states, bed, background_state, ice_mask, flow_rate, obs_cell, obs_value):
    slices, rows, cols = states.shape
    obs = obs_cell.shape[-1]
    group = lax.axis_size("tm")
    cut = cols // group
    width = cut + 2 * HALO
    lanes = -(-slices * width // LANES) * LANES
    full = rows + 2 * HALO
    f32 = lambda *shape: jax.ShapeDtypeStruct(shape, jnp.float32)
    vmem = lambda *shape: pltpu.VMEM(shape, jnp.float32)

    cells = obs_cell.reshape(slices, obs)
    values = obs_value.reshape(slices, obs)
    listed = jnp.stack([cells.astype(jnp.float32), values], axis=1)
    raw = jnp.concatenate(
        [
            states.reshape(slices * rows, cols),
            bed,
            background_state,
            ice_mask.astype(jnp.float32),
            flow_rate,
            listed.reshape(-1, LANES),
        ],
        axis=0,
    )
    near = [lax.ppermute(raw, "gy", pairs) for pairs in neighbour_swaps("gy")]
    dims = (slices, rows, cols, obs, group, len(near), cut, width, lanes)
    *blocks, statics = call(
        functools.partial(pack_kernel, dims),
        [f32(3, rows, lanes)] * group + [f32(4, rows, lanes)],
        [states, bed, background_state, ice_mask, flow_rate, cells, values, *near],
    )
    blocks = [blocks[0]] + [exchange(blocks[k], "tm", k) for k in range(1, group)]
    swaps = neighbour_swaps("gx")
    edges = []
    if swaps:
        sends = call(
            functools.partial(edge_kernel, (group, rows)),
            [f32(3 * group + 4, HALO, lanes)] * len(swaps),
            [*blocks, statics],
        )
        edges = [lax.ppermute(send, "gx", pairs) for send, pairs in zip(sends, swaps)]
    packed = call(
        functools.partial(main_kernel, (slices, rows, group, len(edges), cut, width, lanes)),
        [f32(rows, LANES)] * group,
        [*blocks, statics, *edges],
        [vmem(group, full, lanes)] * 3
        + [vmem(4, full, lanes)]
        + [vmem(group, full, lanes)] * 2
        + [vmem(group, STEPS, 4, full, lanes), vmem(2, full, lanes), vmem(4, full, lanes)],
    )
    pieces = [packed[0]] + [exchange(packed[k], "tm", k) for k in range(1, group)]
    return tuple(
        call(
            functools.partial(join_kernel, (slices, rows, group, cut)),
            [f32(slices, rows, cols), f32(rows, cols)],
            pieces,
        )
    )


def solution(mesh):
    placed = (
        P("tm", "gx", "gy"),
        P("gx", "gy"),
        P("gx", "gy"),
        P("gx", "gy"),
        P("gx", "gy"),
        P("tm", "gx", "gy", None),
        P("tm", "gx", "gy", None),
    )
    return jax.shard_map(
        per_device,
        mesh=mesh,
        in_specs=placed,
        out_specs=(P("tm", "gx", "gy"), P("gx", "gy")),
        check_vma=False,
    )
```

```python
import functools

import jax
import jax.numpy as jnp
from jax import lax
from jax.experimental import pallas as pl
from jax.experimental.pallas import tpu as pltpu
from jax.sharding import PartitionSpec as P

STEPS = 4
OUTER = 2
HALO = 2 * STEPS * OUTER
LANES = 128

bed_rate = 0.1
state_rate = 0.5


def partner(index, shift, count):
    if count & (count - 1) == 0:
        return index ^ shift
    return (index + shift) % count


def source(index, shift, count):
    if count & (count - 1) == 0:
        return index ^ shift
    return (index + count - shift) % count


def exchange(value, axis, shift):
    count = lax.axis_size(axis)
    return lax.ppermute(value, axis, [(i, partner(i, shift, count)) for i in range(count)])


def neighbour_swaps(axis):
    count = lax.axis_size(axis)
    if count == 1:
        return []
    first = [(i, i ^ 1) for i in range(count)]
    if count == 2:
        return [first]
    second = []
    for i in range(1, count, 2):
        j = (i + 1) % count
        second += [(i, j), (j, i)]
    return [first, second]


def call(kernel, out_shape, operands, scratch=(), inputs=pltpu.VMEM):
    spec = pl.BlockSpec(memory_space=pltpu.VMEM)
    return pl.pallas_call(
        kernel,
        out_shape=out_shape,
        in_specs=[pl.BlockSpec(memory_space=inputs)] * len(operands),
        out_specs=jax.tree.map(lambda _: spec, out_shape),
        scratch_shapes=list(scratch),
        name=kernel.func.__name__,
        compiler_params=pltpu.CompilerParams(vmem_limit_bytes=16 << 20),
    )(*operands)


def lane_of(shape):
    return lax.broadcasted_iota(jnp.int32, shape, len(shape) - 1)


def near_first(even, number):
    return even if number == 0 else jnp.logical_not(even)


def copy_kernel(dims, *refs):
    slices, rows, cols, lists, sides = dims
    states, bed, back, mask, rate, cells, values = refs[:7]
    own = refs[7]
    sends = refs[8 : 8 + sides]
    mask_in, cells_in, sems = refs[8 + sides :]
    top = (slices + 4) * rows
    pairs = [(states.at[s], own.at[s * rows : (s + 1) * rows]) for s in range(slices)]
    for i, ref in ((0, bed), (1, back), (3, rate)):
        pairs.append((ref, own.at[(slices + i) * rows : (slices + i + 1) * rows]))
    pairs += [(mask, mask_in), (cells, cells_in), (values, own.at[top + lists : top + 2 * lists])]
    copies = [pltpu.make_async_copy(a, b, sems.at[i]) for i, (a, b) in enumerate(pairs)]
    for copy in copies:
        copy.start()
    for copy in copies:
        copy.wait()
    own[(slices + 2) * rows : (slices + 3) * rows] = mask_in[...].astype(jnp.float32)
    own[top : top + lists] = cells_in[...].astype(jnp.float32)
    even = (lax.axis_index("gy") & 1) == 0
    lane = lane_of((rows, LANES))
    for i, send in enumerate(sends):
        first = jnp.where(near_first(even, i), cols - HALO, 0)
        out = jnp.zeros((rows, LANES), jnp.float32)
        for j in range(slices + 4):
            shift = (HALO * j - first + 2 * LANES) % LANES
            moved = pltpu.roll(own[j * rows : (j + 1) * rows], shift, 1)
            out = jnp.where((lane >= HALO * j) & (lane < HALO * (j + 1)), moved, out)
        send[0:rows] = out
        send[rows : rows + 2 * lists] = own[top : top + 2 * lists]


def pack_kernel(dims, *refs):
    slices, rows, cols, lists, group, sides, cut, width = dims
    own = refs[0]
    near = refs[1 : 1 + sides]
    blocks = refs[1 + sides : 1 + sides + group]
    statics = refs[1 + sides + group]
    me = lax.axis_index("tm")
    y = lax.axis_index("gy")
    last_y = lax.axis_size("gy") - 1
    lane = lane_of((rows, LANES))
    even = (y & 1) == 0
    top = (slices + 4) * rows

    def placed(number, start, offset):
        column = lane - offset + start
        shift = offset - start + 4 * LANES
        value = pltpu.roll(own[number * rows : (number + 1) * rows], shift % LANES, 1)
        for i, ref in enumerate(near):
            after = near_first(even, i)
            there = pltpu.roll(ref[0:rows], (shift - HALO * number + jnp.where(after, cols, -HALO)) % LANES, 1)
            if sides == 1:
                beyond = (column < 0) | (column >= cols)
            else:
                beyond = ((column >= cols) & after) | ((column < 0) & jnp.logical_not(after))
            value = jnp.where(beyond, there, value)
        if number == slices + 2:
            left = (column < 0) & (y == 0)
            right = (column >= cols) & (y == last_y)
            value = jnp.where(left | right, 0.0, value)
        return value

    def packed(numbers, start):
        out = placed(numbers[0], start, 0)
        for s, number in enumerate(numbers[1:], 1):
            out = jnp.where(lane >= s * width, placed(number, start, s * width), out)
        return out

    for k in range(group):
        start = partner(me, k, group) * cut - HALO
        blocks[k][0:rows] = packed(list(range(slices)), start)
        blocks[k][rows : rows + 2 * lists] = own[top : top + 2 * lists]
        for i, ref in enumerate(near):
            low = rows + 2 * lists * (i + 1)
            blocks[k][low : low + 2 * lists] = ref[rows : rows + 2 * lists]
    start = me * cut - HALO
    statics[0] = packed([slices, slices + 1], start)
    statics[1] = packed([slices + 2, slices + 3], start)


def maps_kernel(dims, *refs):
    slices, rows, cols, lists, group, sides, cut, width = dims
    blocks, statics = refs[:group], refs[group]
    maps = refs[group + 1]
    sends = refs[group + 2 :]
    start = lax.axis_index("tm") * cut - HALO
    even = (lax.axis_index("gy") & 1) == 0
    each = lists // slices
    for k in range(group):
        found = [[], []]
        for s in range(slices):
            row, col, value = [], [], []
            for side in range(1 + sides):
                low = rows + 2 * lists * side + each * s
                shift = -start
                if side:
                    shift = shift + jnp.where(near_first(even, side - 1), cols, -cols)
                for j in range(each):
                    cell = blocks[k][low + j : low + j + 1].astype(jnp.int32)
                    row.append(cell // cols)
                    col.append(cell % cols + shift)
                    value.append(blocks[k][low + lists + j : low + lists + j + 1])
            row, col, value = (jnp.concatenate(v, axis=1) for v in (row, col, value))
            n = row.shape[1]
            at_row = lax.broadcasted_iota(jnp.int32, (rows, n), 0) == row
            at_col = lax.broadcasted_iota(jnp.int32, (width, n), 0) == col
            left = jnp.where(at_row, 1.0, 0.0).astype(jnp.bfloat16)
            part1 = value.astype(jnp.bfloat16).astype(jnp.float32)
            rest = value - part1
            part2 = rest.astype(jnp.bfloat16).astype(jnp.float32)
            weights = (jnp.ones_like(value), part1, part2, rest - part2)
            right = jnp.concatenate([jnp.where(at_col, w, 0.0).astype(jnp.bfloat16) for w in weights], axis=0)
            out = lax.dot_general(left, right, (((1,), (1,)), ((), ())), preferred_element_type=jnp.float32)
            found[0].append(out[:, 0:width])
            found[1].append(out[:, width : 2 * width] + (out[:, 2 * width : 3 * width] + out[:, 3 * width : 4 * width]))
        for i in range(2):
            parts = found[i]
            if slices * width < LANES:
                parts = parts + [jnp.zeros((rows, LANES - slices * width), jnp.float32)]
            maps[2 * k + i] = jnp.concatenate(parts, axis=1)
    even = (lax.axis_index("gx") & 1) == 0
    for i, send in enumerate(sends):
        low = pl.multiple_of(jnp.where(near_first(even, i), rows - HALO, 0), 8)
        for k in range(group):
            send[k] = blocks[k][pl.ds(low, HALO)]
        send[group : 3 * group] = maps[:, pl.ds(low, HALO)]
        send[3 * group : 3 * group + 2] = statics[:, pl.ds(low, HALO)]


def main_kernel(dims, *refs):
    slices, rows, group, sides, cut, width = dims
    blocks, statics, maps = refs[:group], refs[group], refs[group + 1]
    edges = refs[group + 2 : group + 2 + sides]
    outs = refs[group + 2 + sides : 2 * group + 2 + sides]
    state, count, total, fixed, final, misfit, keep, coef = refs[2 * group + 2 + sides :]
    me = lax.axis_index("tm")
    x = lax.axis_index("gx")
    last_x = lax.axis_size("gx") - 1
    even = (x & 1) == 0
    full = rows + 2 * HALO
    wrap = (slices - 1) * width

    def put(target, main, pieces):
        target[HALO : HALO + rows] = main
        if sides < 2:
            target[0:HALO] = jnp.zeros((HALO, LANES), jnp.float32)
            target[HALO + rows : full] = jnp.zeros((HALO, LANES), jnp.float32)
        for i, piece in enumerate(pieces):
            after = near_first(even, i)
            target[pl.ds(pl.multiple_of(jnp.where(after, HALO + rows, 0), 8), HALO)] = piece

    for k in range(group):
        pair = source(me, k, group)
        put(state.at[pair], blocks[k][0:rows], [e[k] for e in edges])
        put(count.at[pair], maps[2 * k], [e[group + 2 * k] for e in edges])
        put(total.at[pair], maps[2 * k + 1], [e[group + 2 * k + 1] for e in edges])
    for i in range(2):
        put(fixed.at[i], statics[i], [e[3 * group + i] for e in edges])

    row = lax.broadcasted_iota(jnp.int32, (full, LANES), 0)
    lane = lane_of((full, LANES))
    down = lambda v: pltpu.roll(v, v.shape[0] - 1, 0)
    up = lambda v: pltpu.roll(v, 1, 0)
    right = lambda v: pltpu.roll(v, LANES - 1, 1)
    left = lambda v: pltpu.roll(v, 1, 1)
    moves = ((down, up), (right, left))

    def spread(value):
        out = value
        for s in range(1, slices):
            out = jnp.where(lane[: value.shape[0]] >= s * width, pltpu.roll(value, s * width, 1), out)
        return out

    second = lambda v: pltpu.roll(v, LANES - width, 1)
    outside = ((row < HALO) & (x == 0)) | ((row >= HALO + rows) & (x == last_x))
    mask = jnp.where(outside, 0.0, spread(fixed[1]))
    rate = spread(second(fixed[1]))
    prior = spread(fixed[0])
    background = second(fixed[0])
    seam = lane % width == width - 1
    if LANES != slices * width:
        seam = seam | (lane >= slices * width)
    coef[0] = 0.25 * (rate + down(rate)) * (mask * down(mask))
    coef[1] = jnp.where(seam, 0.0, 0.25 * (rate + right(rate)) * (mask * right(mask)))
    fixed[0] = prior
    fixed[1] = background
    fixed[2] = prior

    pairs = range(group)
    for outer in range(OUTER):
        low = 2 * STEPS * outer
        high = full - low
        size = high - low
        span = pl.ds(low, size)
        here = lane[:size]
        bed = fixed[2, span]
        coef[0, span] = jnp.where(row[:size] == size - 1, 0.0, coef[0, span])
        coef[2, span] = down(bed) - bed
        coef[3, span] = right(bed) - bed

        thick = [state[p, span] for p in pairs]
        for step in range(STEPS):
            fluxes = []
            for d, (ahead, behind) in enumerate(moves):
                there = [ahead(v) for v in thick]
                flux = []
                for p in pairs:
                    both = thick[p] + there[p]
                    slope = (there[p] - thick[p]) + coef[2 + d, span]
                    scaled = coef[d, span] * both
                    half = 0.5 * both
                    by_mean = scaled * slope
                    keep[p, step, 2 * d, span] = half * scaled
                    keep[p, step, 2 * d + 1, span] = by_mean
                    flux.append(half * by_mean)
                fluxes.append((flux, [behind(v) for v in flux]))
            thick = [
                thick[p] + ((fluxes[0][0][p] - fluxes[0][1][p]) + (fluxes[1][0][p] - fluxes[1][1][p])) for p in pairs
            ]
        for p in pairs:
            final[p, span] = thick[p]

        for p in pairs:
            own = final[p, span]
            start = pltpu.roll(final[p - 1, span], (LANES - wrap) % LANES, 1) if p else fixed[1, span]
            earlier = jnp.where(here < width, start, pltpu.roll(own, width, 1))
            misfit[p, span] = state[p, span] - earlier
        pull = []
        for p in pairs:
            later = pltpu.roll(misfit[p, span], LANES - width, 1)
            after = pltpu.roll(misfit[p + 1, span], wrap, 1) if p + 1 < group else 0.0
            later = jnp.where(here < wrap, later, after)
            pull.append(count[p, span] * final[p, span] - total[p, span] - later)

        sums = [None, None]
        for step in reversed(range(STEPS)):
            parts = []
            for d, (ahead, behind) in enumerate(moves):
                jump = [v - ahead(v) for v in pull]
                own, passed = [], []
                for p in pairs:
                    by_slope = keep[p, step, 2 * d, span] * jump[p]
                    by_mean = keep[p, step, 2 * d + 1, span] * jump[p]
                    sums[d] = by_slope if sums[d] is None else sums[d] + by_slope
                    own.append(by_mean - by_slope)
                    passed.append(by_mean + by_slope)
                parts.append((own, [behind(v) for v in passed]))
            pull = [pull[p] + ((parts[0][0][p] + parts[0][1][p]) + (parts[1][0][p] + parts[1][1][p])) for p in pairs]
        for p in pairs:
            state[p, span] = state[p, span] - state_rate * (misfit[p, span] + pull[p])
        by_x, by_y = sums
        each = (up(by_x) - by_x) + (left(by_y) - by_y)
        summed = each
        for s in range(1, slices):
            summed = summed + pltpu.roll(each, LANES - s * width, 1)
        fixed[2, span] = bed - bed_rate * (spread(summed) + (bed - prior[low:high]))

    inner = slice(HALO, HALO + rows)

    def fold(value, used):
        parts = LANES // used
        height = value.shape[0] // parts
        out = value[0:height]
        place = lane_of((height, LANES))
        for i in range(1, parts):
            moved = pltpu.roll(value[i * height : (i + 1) * height], i * used, 1)
            out = jnp.where(place >= i * used, moved, out)
        return out

    place = lane_of((rows, LANES))
    ground = fold(pltpu.roll(fixed[2, inner], LANES - HALO, 1), cut)
    for k in range(group):
        mine = state[partner(me, k, group), inner]
        out = pltpu.roll(mine, LANES - HALO, 1)
        for s in range(1, slices):
            out = jnp.where(place >= s * cut, pltpu.roll(mine, (s * cut - s * width - HALO) % LANES, 1), out)
        folded = fold(out, slices * cut)
        outs[k][0 : folded.shape[0]] = folded
        outs[k][folded.shape[0] :] = ground


def join_kernel(dims, *refs):
    slices, rows, group, cut = dims
    pieces, states, bed = refs[:group], refs[group], refs[group + 1]
    me = lax.axis_index("tm")
    height = rows * slices * cut // LANES
    for target, used, low, count in [(states.at[s], slices * cut, s * cut, height) for s in range(slices)] + [
        (bed, cut, 0, rows * cut // LANES)
    ]:
        base = 0 if count == height and target is not bed else height
        lane = lane_of((count, LANES))
        for i in range(LANES // used):
            out = jnp.zeros((count, LANES), jnp.float32)
            for k in range(group):
                first = source(me, k, group) * cut
                moved = pltpu.roll(pieces[k][base : base + count], (first - i * used - low + 2 * LANES) % LANES, 1)
                out = jnp.where((lane >= first) & (lane < first + cut), moved, out)
            target[i * count : (i + 1) * count] = out


def per_device(states, bed, background_state, ice_mask, flow_rate, obs_cell, obs_value):
    slices, rows, cols = states.shape
    group = lax.axis_size("tm")
    cut = cols // group
    width = cut + 2 * HALO
    full = rows + 2 * HALO
    lists = slices * obs_cell.shape[-1] // LANES
    f32 = lambda *shape: jax.ShapeDtypeStruct(shape, jnp.float32)
    vmem = lambda *shape: pltpu.VMEM(shape, jnp.float32)

    swaps_y = neighbour_swaps("gy")
    sides = len(swaps_y)
    own, *sends = call(
        functools.partial(copy_kernel, (slices, rows, cols, lists, sides)),
        [f32((slices + 4) * rows + 2 * lists, cols)] + [f32(rows + 2 * lists, LANES)] * sides,
        [pltpu.with_memory_space_constraint(v, pltpu.HBM) for v in (states, bed, background_state, ice_mask, flow_rate, obs_cell.reshape(lists, LANES), obs_value.reshape(lists, LANES))],
        [pltpu.VMEM((rows, cols), jnp.int32), pltpu.VMEM((lists, LANES), jnp.int32), pltpu.SemaphoreType.DMA((slices + 6,))],
        inputs=pltpu.HBM,
    )
    near = [lax.ppermute(send, "gy", pairs) for send, pairs in zip(sends, swaps_y)]
    dims = (slices, rows, cols, lists, group, sides, cut, width)
    *blocks, statics = call(
        functools.partial(pack_kernel, dims),
        [f32(rows + 2 * lists * (1 + sides), LANES)] * group + [f32(2, rows, LANES)],
        [own, *near],
    )
    blocks = [blocks[0]] + [exchange(blocks[k], "tm", k) for k in range(1, group)]
    swaps_x = neighbour_swaps("gx")
    maps, *sends = call(
        functools.partial(maps_kernel, dims),
        [f32(2 * group, rows, LANES)] + [f32(3 * group + 2, HALO, LANES)] * len(swaps_x),
        [*blocks, statics],
    )
    edges = [lax.ppermute(send, "gx", pairs) for send, pairs in zip(sends, swaps_x)]
    packed = call(
        functools.partial(main_kernel, (slices, rows, group, len(edges), cut, width)),
        [f32(rows * (slices + 1) * cut // LANES, LANES)] * group,
        [*blocks, statics, maps, *edges],
        [vmem(group, full, LANES)] * 3
        + [vmem(3, full, LANES)]
        + [vmem(group, full, LANES)] * 2
        + [vmem(group, STEPS, 4, full, LANES), vmem(4, full, LANES)],
    )
    pieces = [packed[0]] + [exchange(packed[k], "tm", k) for k in range(1, group)]
    return tuple(
        call(
            functools.partial(join_kernel, (slices, rows, group, cut)),
            [f32(slices, rows, cols), f32(rows, cols)],
            pieces,
        )
    )


def solution(mesh):
    placed = (
        P("tm", "gx", "gy"),
        P("gx", "gy"),
        P("gx", "gy"),
        P("gx", "gy"),
        P("gx", "gy"),
        P("tm", "gx", "gy", None),
        P("tm", "gx", "gy", None),
    )
    return jax.shard_map(
        per_device,
        mesh=mesh,
        in_specs=placed,
        out_specs=(P("tm", "gx", "gy"), P("gx", "gy")),
        check_vma=False,
    )
```

```python
import functools

import jax
import jax.numpy as jnp
from jax import lax
from jax.experimental import pallas as pl
from jax.experimental.pallas import tpu as pltpu
from jax.sharding import PartitionSpec as P


STEPS = 4
OUTER = 2
HALO = 2 * STEPS * OUTER
LANES = 128

bed_rate = 0.1
state_rate = 0.5


def partner(index, number, count):
    shift = (count - number) % count
    if count & (count - 1) == 0:
        return index ^ shift
    return (index + shift) % count


def source(index, number, count):
    shift = (count - number) % count
    if count & (count - 1) == 0:
        return index ^ shift
    return (index + count - shift) % count


def exchange(value, axis, number):
    count = lax.axis_size(axis)
    return lax.ppermute(value, axis, [(i, partner(i, number, count)) for i in range(count)])


def neighbour_swaps(axis):
    count = lax.axis_size(axis)
    if count == 1:
        return []
    near = [(i, i ^ 1) for i in range(count)]
    if count == 2:
        return [near]
    far = []
    for i in range(1, count, 2):
        j = (i + 1) % count
        far += [(i, j), (j, i)]
    return [far, near]


def reaches_after(index, number, swaps):
    return (index & 1) == (0 if number == swaps - 1 else 1)


def exchange_all(values):
    out = list(values)
    for k in range(1, len(values)):
        out[k] = exchange(values[k], "tm", k)
    return out


def swap_all(values, axis):
    out = []
    for value, pairs in zip(values, neighbour_swaps(axis)):
        out.append(lax.ppermute(value, axis, pairs))
    return out


def call(kernel, out_shape, operands, scratch=(), inputs=pltpu.VMEM, cost=None):
    spec = pl.BlockSpec(memory_space=pltpu.VMEM)
    return pl.pallas_call(
        kernel,
        out_shape=out_shape,
        in_specs=[pl.BlockSpec(memory_space=inputs)] * len(operands),
        out_specs=jax.tree.map(lambda _: spec, out_shape),
        scratch_shapes=list(scratch),
        cost_estimate=cost,
        compiler_params=pltpu.CompilerParams(vmem_limit_bytes=16 << 20),
    )(*operands)


def lane_of(shape):
    return lax.broadcasted_iota(jnp.int32, shape, len(shape) - 1)


def copy_kernel(dims, *refs):
    slices, rows, cols, lists, sides = dims
    states, bed, back, mask, rate, cells, values = refs[:7]
    own = refs[7]
    sends = refs[8 : 8 + sides]
    mask_in, cells_in, sems = refs[8 + sides :]
    top = (slices + 4) * rows
    pairs = [(states.at[s], own.at[s * rows : (s + 1) * rows]) for s in range(slices)]
    for i, ref in ((0, bed), (1, back), (3, rate)):
        pairs.append((ref, own.at[(slices + i) * rows : (slices + i + 1) * rows]))
    pairs += [(mask, mask_in), (cells, cells_in), (values, own.at[top + lists : top + 2 * lists])]
    copies = [pltpu.make_async_copy(a, b, sems.at[i]) for i, (a, b) in enumerate(pairs)]
    for copy in copies:
        copy.start()
    for copy in copies:
        copy.wait()
    own[(slices + 2) * rows : (slices + 3) * rows] = mask_in[...].astype(jnp.float32)
    own[top : top + lists] = cells_in[...].astype(jnp.float32)
    y = lax.axis_index("gy")
    lane = lane_of((rows, LANES))
    for i, send in enumerate(sends):
        first = jnp.where(reaches_after(y, i, sides), cols - HALO, 0)
        out = jnp.zeros((rows, LANES), jnp.float32)
        for j in range(slices + 4):
            shift = (HALO * j - first + 2 * LANES) % LANES
            moved = pltpu.roll(own[j * rows : (j + 1) * rows], shift, 1)
            out = jnp.where((lane >= HALO * j) & (lane < HALO * (j + 1)), moved, out)
        send[0:rows] = out
        send[rows : rows + 2 * lists] = own[top : top + 2 * lists]


def pack_kernel(dims, *refs):
    slices, rows, cols, lists, group, sides, cut, width = dims
    own = refs[0]
    near = refs[1 : 1 + sides]
    blocks = refs[1 + sides : 1 + sides + group]
    statics = refs[1 + sides + group]
    me = lax.axis_index("tm")
    y = lax.axis_index("gy")
    last_y = lax.axis_size("gy") - 1
    lane = lane_of((rows, LANES))
    top = (slices + 4) * rows

    def placed(number, start, offset):
        column = lane - offset + start
        shift = offset - start + 4 * LANES
        value = pltpu.roll(own[number * rows : (number + 1) * rows], shift % LANES, 1)
        for i, ref in enumerate(near):
            after = reaches_after(y, i, sides)
            there = pltpu.roll(ref[0:rows], (shift - HALO * number + jnp.where(after, cols, -HALO)) % LANES, 1)
            if sides == 1:
                beyond = (column < 0) | (column >= cols)
            else:
                beyond = ((column >= cols) & after) | ((column < 0) & jnp.logical_not(after))
            value = jnp.where(beyond, there, value)
        if number == slices + 2:
            left = (column < 0) & (y == 0)
            right = (column >= cols) & (y == last_y)
            value = jnp.where(left | right, 0.0, value)
        return value

    def packed(numbers, start):
        out = placed(numbers[0], start, 0)
        for s, number in enumerate(numbers[1:], 1):
            out = jnp.where(lane >= s * width, placed(number, start, s * width), out)
        return out

    for k in range(group):
        start = partner(me, k, group) * cut - HALO
        blocks[k][0:rows] = packed(list(range(slices)), start)
        blocks[k][rows : rows + 2 * lists] = own[top : top + 2 * lists]
        for i, ref in enumerate(near):
            low = rows + 2 * lists * (i + 1)
            blocks[k][low : low + 2 * lists] = ref[rows : rows + 2 * lists]
    start = me * cut - HALO
    statics[0] = packed([slices, slices + 1], start)
    statics[1] = packed([slices + 2, slices + 3], start)


def maps_kernel(dims, block, maps):
    slices, rows, cols, lists, _, sides, cut, width = dims
    start = lax.axis_index("tm") * cut - HALO
    y = lax.axis_index("gy")
    each = lists // slices
    found = [[], []]
    for s in range(slices):
        row, col, value = [], [], []
        for side in range(1 + sides):
            low = rows + 2 * lists * side + each * s
            shift = -start
            if side:
                shift = shift + jnp.where(reaches_after(y, side - 1, sides), cols, -cols)
            for j in range(each):
                cell = block[low + j : low + j + 1].astype(jnp.int32)
                row.append(cell // cols)
                col.append(cell % cols + shift)
                value.append(block[low + lists + j : low + lists + j + 1])
        row, col, value = (jnp.concatenate(v, axis=1) for v in (row, col, value))
        n = row.shape[1]
        at_row = lax.broadcasted_iota(jnp.int32, (rows, n), 0) == row
        at_col = lax.broadcasted_iota(jnp.int32, (width, n), 0) == col
        left = jnp.where(at_row, 1.0, 0.0).astype(jnp.bfloat16)
        part1 = value.astype(jnp.bfloat16).astype(jnp.float32)
        rest = value - part1
        part2 = rest.astype(jnp.bfloat16).astype(jnp.float32)
        weights = (jnp.ones_like(value), part1, part2, rest - part2)
        right = jnp.concatenate([jnp.where(at_col, w, 0.0).astype(jnp.bfloat16) for w in weights], axis=0)
        out = lax.dot_general(left, right, (((1,), (1,)), ((), ())), preferred_element_type=jnp.float32)
        found[0].append(out[:, 0:width])
        found[1].append(out[:, width : 2 * width] + (out[:, 2 * width : 3 * width] + out[:, 3 * width : 4 * width]))
    for i in range(2):
        parts = found[i]
        if slices * width < LANES:
            parts = parts + [jnp.zeros((rows, LANES - slices * width), jnp.float32)]
        maps[i] = jnp.concatenate(parts, axis=1)


def edge_kernel(dims, *refs):
    rows, group = dims
    blocks, statics = refs[:group], refs[group]
    maps = refs[group + 1 : 2 * group + 1]
    sends = refs[2 * group + 1 :]
    x = lax.axis_index("gx")
    for i, send in enumerate(sends):
        low = pl.multiple_of(jnp.where(reaches_after(x, i, len(sends)), rows - HALO, 0), 8)
        for k in range(group):
            send[k] = blocks[k][pl.ds(low, HALO)]
            send[group + 2 * k : group + 2 * k + 2] = maps[k][:, pl.ds(low, HALO)]
        send[3 * group : 3 * group + 2] = statics[:, pl.ds(low, HALO)]


def main_kernel(dims, *refs):
    slices, rows, group, sides, cut, width = dims
    blocks, statics, maps = refs[:group], refs[group], refs[group + 1 : 2 * group + 1]
    edges = refs[2 * group + 1 : 2 * group + 1 + sides]
    outs = refs[2 * group + 1 + sides : 3 * group + 1 + sides]
    state, count, total, fixed, final, misfit, keep, coef = refs[3 * group + 1 + sides :]
    me = lax.axis_index("tm")
    x = lax.axis_index("gx")
    last_x = lax.axis_size("gx") - 1
    full = rows + 2 * HALO
    wrap = (slices - 1) * width

    def put(target, main, pieces):
        target[HALO : HALO + rows] = main
        if sides < 2:
            target[0:HALO] = jnp.zeros((HALO, LANES), jnp.float32)
            target[HALO + rows : full] = jnp.zeros((HALO, LANES), jnp.float32)
        for i, piece in enumerate(pieces):
            after = reaches_after(x, i, sides)
            target[pl.ds(pl.multiple_of(jnp.where(after, HALO + rows, 0), 8), HALO)] = piece

    for k in range(group):
        pair = source(me, k, group)
        put(state.at[pair], blocks[k][0:rows], [e[k] for e in edges])
        put(count.at[pair], maps[k][0], [e[group + 2 * k] for e in edges])
        put(total.at[pair], maps[k][1], [e[group + 2 * k + 1] for e in edges])
    for i in range(2):
        put(fixed.at[i], statics[i], [e[3 * group + i] for e in edges])

    row = lax.broadcasted_iota(jnp.int32, (full, LANES), 0)
    lane = lane_of((full, LANES))
    down = lambda v: pltpu.roll(v, v.shape[0] - 1, 0)
    up = lambda v: pltpu.roll(v, 1, 0)
    right = lambda v: pltpu.roll(v, LANES - 1, 1)
    left = lambda v: pltpu.roll(v, 1, 1)
    moves = ((down, up), (right, left))

    def spread(value):
        out = value
        for s in range(1, slices):
            out = jnp.where(lane[: value.shape[0]] >= s * width, pltpu.roll(value, s * width, 1), out)
        return out

    second = lambda v: pltpu.roll(v, LANES - width, 1)
    outside = ((row < HALO) & (x == 0)) | ((row >= HALO + rows) & (x == last_x))
    mask = jnp.where(outside, 0.0, spread(fixed[1]))
    rate = spread(second(fixed[1]))
    prior = spread(fixed[0])
    background = second(fixed[0])
    seam = lane % width == width - 1
    if LANES != slices * width:
        seam = seam | (lane >= slices * width)
    coef[0] = 0.25 * (rate + down(rate)) * (mask * down(mask))
    coef[1] = jnp.where(seam, 0.0, 0.25 * (rate + right(rate)) * (mask * right(mask)))
    fixed[0] = prior
    fixed[1] = background
    fixed[2] = prior

    pairs = range(group)
    for outer in range(OUTER):
        low = 2 * STEPS * outer
        high = full - low
        size = high - low
        span = pl.ds(low, size)
        here = lane[:size]
        bed = fixed[2, span]
        coef[0, span] = jnp.where(row[:size] == size - 1, 0.0, coef[0, span])
        coef[2, span] = down(bed) - bed
        coef[3, span] = right(bed) - bed

        thick = [state[p, span] for p in pairs]
        for step in range(STEPS):
            fluxes = []
            for d, (ahead, behind) in enumerate(moves):
                there = [ahead(v) for v in thick]
                flux = []
                for p in pairs:
                    both = thick[p] + there[p]
                    slope = (there[p] - thick[p]) + coef[2 + d, span]
                    scaled = coef[d, span] * both
                    half = 0.5 * both
                    by_mean = scaled * slope
                    keep[p, step, 2 * d, span] = half * scaled
                    keep[p, step, 2 * d + 1, span] = by_mean
                    flux.append(half * by_mean)
                fluxes.append((flux, [behind(v) for v in flux]))
            thick = [
                thick[p] + ((fluxes[0][0][p] - fluxes[0][1][p]) + (fluxes[1][0][p] - fluxes[1][1][p])) for p in pairs
            ]
        for p in pairs:
            final[p, span] = thick[p]

        for p in pairs:
            own = final[p, span]
            start = pltpu.roll(final[p - 1, span], (LANES - wrap) % LANES, 1) if p else fixed[1, span]
            earlier = jnp.where(here < width, start, pltpu.roll(own, width, 1))
            misfit[p, span] = state[p, span] - earlier
        pull = []
        for p in pairs:
            later = pltpu.roll(misfit[p, span], LANES - width, 1)
            after = pltpu.roll(misfit[p + 1, span], wrap, 1) if p + 1 < group else 0.0
            later = jnp.where(here < wrap, later, after)
            pull.append(count[p, span] * final[p, span] - total[p, span] - later)

        sums = [None, None]
        for step in reversed(range(STEPS)):
            parts = []
            for d, (ahead, behind) in enumerate(moves):
                jump = [v - ahead(v) for v in pull]
                own, passed = [], []
                for p in pairs:
                    by_slope = keep[p, step, 2 * d, span] * jump[p]
                    by_mean = keep[p, step, 2 * d + 1, span] * jump[p]
                    sums[d] = by_slope if sums[d] is None else sums[d] + by_slope
                    own.append(by_mean - by_slope)
                    passed.append(by_mean + by_slope)
                parts.append((own, [behind(v) for v in passed]))
            pull = [pull[p] + ((parts[0][0][p] + parts[0][1][p]) + (parts[1][0][p] + parts[1][1][p])) for p in pairs]
        for p in pairs:
            state[p, span] = state[p, span] - state_rate * (misfit[p, span] + pull[p])
        by_x, by_y = sums
        each = (up(by_x) - by_x) + (left(by_y) - by_y)
        summed = each
        for s in range(1, slices):
            summed = summed + pltpu.roll(each, LANES - s * width, 1)
        fixed[2, span] = bed - bed_rate * (spread(summed) + (bed - prior[low:high]))

    inner = slice(HALO, HALO + rows)

    def fold(value, used):
        parts = LANES // used
        height = value.shape[0] // parts
        out = value[0:height]
        place = lane_of((height, LANES))
        for i in range(1, parts):
            moved = pltpu.roll(value[i * height : (i + 1) * height], i * used, 1)
            out = jnp.where(place >= i * used, moved, out)
        return out

    place = lane_of((rows, LANES))
    ground = fold(pltpu.roll(fixed[2, inner], LANES - HALO, 1), cut)
    for k in range(group):
        mine = state[partner(me, k, group), inner]
        out = pltpu.roll(mine, LANES - HALO, 1)
        for s in range(1, slices):
            out = jnp.where(place >= s * cut, pltpu.roll(mine, (s * cut - s * width - HALO) % LANES, 1), out)
        folded = fold(out, slices * cut)
        outs[k][0 : folded.shape[0]] = folded
        outs[k][folded.shape[0] :] = ground


def join_kernel(dims, *refs):
    slices, rows, group, cut = dims
    pieces, states, bed = refs[:group], refs[group], refs[group + 1]
    me = lax.axis_index("tm")
    height = rows * slices * cut // LANES
    for target, used, low, count in [(states.at[s], slices * cut, s * cut, height) for s in range(slices)] + [
        (bed, cut, 0, rows * cut // LANES)
    ]:
        base = 0 if count == height and target is not bed else height
        lane = lane_of((count, LANES))
        for i in range(LANES // used):
            out = jnp.zeros((count, LANES), jnp.float32)
            for k in range(group):
                first = source(me, k, group) * cut
                moved = pltpu.roll(pieces[k][base : base + count], (first - i * used - low + 2 * LANES) % LANES, 1)
                out = jnp.where((lane >= first) & (lane < first + cut), moved, out)
            target[i * count : (i + 1) * count] = out


def step(states, bed, background_state, ice_mask, flow_rate, obs_cell, obs_value):
    slices, rows, cols = states.shape
    group = lax.axis_size("tm")
    cut = cols // group
    width = cut + 2 * HALO
    full = rows + 2 * HALO
    lists = slices * obs_cell.shape[-1] // LANES
    f32 = lambda *shape: jax.ShapeDtypeStruct(shape, jnp.float32)
    vmem = lambda *shape: pltpu.VMEM(shape, jnp.float32)

    swaps_y = neighbour_swaps("gy")
    sides = len(swaps_y)
    own, *sends = call(
        functools.partial(copy_kernel, (slices, rows, cols, lists, sides)),
        [f32((slices + 4) * rows + 2 * lists, cols)] + [f32(rows + 2 * lists, LANES)] * sides,
        [pltpu.with_memory_space_constraint(v, pltpu.HBM) for v in (states, bed, background_state, ice_mask, flow_rate, obs_cell.reshape(lists, LANES), obs_value.reshape(lists, LANES))],
        [pltpu.VMEM((rows, cols), jnp.int32), pltpu.VMEM((lists, LANES), jnp.int32), pltpu.SemaphoreType.DMA((slices + 6,))],
        inputs=pltpu.HBM,
    )
    near = swap_all(sends, "gy")
    dims = (slices, rows, cols, lists, group, sides, cut, width)
    *blocks, statics = call(
        functools.partial(pack_kernel, dims),
        [f32(rows + 2 * lists * (1 + sides), LANES)] * group + [f32(2, rows, LANES)],
        [own, *near],
    )
    blocks = exchange_all(blocks)
    swaps_x = neighbour_swaps("gx")
    flops = 2 * rows * (lists * LANES * (1 + sides)) * 4 * width
    maps = []
    for block in blocks:
        maps.append(
            call(
                functools.partial(maps_kernel, dims),
                f32(2, rows, LANES),
                [block],
                cost=pl.CostEstimate(flops=flops, bytes_accessed=1 << 20, transcendentals=0),
            )
        )
    sends = call(
        functools.partial(edge_kernel, (rows, group)),
        [f32(3 * group + 2, HALO, LANES)] * len(swaps_x),
        [*blocks, statics, *maps],
    ) if swaps_x else []
    edges = swap_all(sends, "gx")
    packed = call(
        functools.partial(main_kernel, (slices, rows, group, len(edges), cut, width)),
        [f32(rows * (slices + 1) * cut // LANES, LANES)] * group,
        [*blocks, statics, *maps, *edges],
        [vmem(group, full, LANES)] * 3
        + [vmem(3, full, LANES)]
        + [vmem(group, full, LANES)] * 2
        + [vmem(group, STEPS, 4, full, LANES), vmem(4, full, LANES)],
    )
    pieces = exchange_all(packed)
    return tuple(
        call(
            functools.partial(join_kernel, (slices, rows, group, cut)),
            [f32(slices, rows, cols), f32(rows, cols)],
            pieces,
        )
    )


def solution(mesh):
    placed = (
        P("tm", "gx", "gy"),
        P("gx", "gy"),
        P("gx", "gy"),
        P("gx", "gy"),
        P("gx", "gy"),
        P("tm", "gx", "gy", None),
        P("tm", "gx", "gy", None),
    )
    return jax.shard_map(
        step,
        mesh=mesh,
        in_specs=placed,
        out_specs=(P("tm", "gx", "gy"), P("gx", "gy")),
        check_vma=False,
    )
```

```python
import functools

import jax
import jax.numpy as jnp
from jax import lax
from jax.experimental import pallas as pl
from jax.experimental.pallas import tpu as pltpu
from jax.sharding import PartitionSpec as P


STEPS = 4
OUTER = 2
HALO = 2 * STEPS * OUTER
REACH = HALO - STEPS
LANES = 128

bed_rate = 0.1
state_rate = 0.5


def partner(index, number, count):
    shift = (count - number) % count
    if count & (count - 1) == 0:
        return index ^ shift
    return (index + shift) % count


def source(index, number, count):
    shift = (count - number) % count
    if count & (count - 1) == 0:
        return index ^ shift
    return (index + count - shift) % count


def exchange(value, axis, number):
    count = lax.axis_size(axis)
    return lax.ppermute(value, axis, [(i, partner(i, number, count)) for i in range(count)])


def neighbour_swaps(axis):
    count = lax.axis_size(axis)
    if count == 1:
        return []
    near = [(i, i ^ 1) for i in range(count)]
    if count == 2:
        return [near]
    far = []
    for i in range(1, count, 2):
        j = (i + 1) % count
        far += [(i, j), (j, i)]
    return [far, near]


def reaches_after(index, number, swaps):
    return (index & 1) == (0 if number == swaps - 1 else 1)


def exchange_all(values):
    out = list(values)
    for k in range(1, len(values)):
        out[k] = exchange(values[k], "tm", k)
    return out


def swap_all(values, axis):
    out = []
    for value, pairs in zip(values, neighbour_swaps(axis)):
        out.append(lax.ppermute(value, axis, pairs))
    return out


def call(kernel, out_shape, operands, scratch=(), inputs=pltpu.VMEM):
    spec = pl.BlockSpec(memory_space=pltpu.VMEM)
    return pl.pallas_call(
        kernel,
        out_shape=out_shape,
        in_specs=[pl.BlockSpec(memory_space=inputs)] * len(operands),
        out_specs=jax.tree.map(lambda _: spec, out_shape),
        scratch_shapes=list(scratch),
        compiler_params=pltpu.CompilerParams(vmem_limit_bytes=16 << 20),
    )(*operands)


def lane_of(shape):
    return lax.broadcasted_iota(jnp.int32, shape, len(shape) - 1)


def copy_kernel(dims, *refs):
    slices, rows, cols, lists, sides = dims
    states, bed, back, mask, rate, cells, values = refs[:7]
    own = refs[7]
    sends = refs[8 : 8 + sides]
    mask_in, cells_in, sems = refs[8 + sides :]
    top = (slices + 4) * rows
    pairs = [(states.at[s], own.at[s * rows : (s + 1) * rows]) for s in range(slices)]
    for i, ref in ((0, bed), (1, back), (3, rate)):
        pairs.append((ref, own.at[(slices + i) * rows : (slices + i + 1) * rows]))
    pairs += [(mask, mask_in), (cells, cells_in), (values, own.at[top + lists : top + 2 * lists])]
    copies = [pltpu.make_async_copy(a, b, sems.at[i]) for i, (a, b) in enumerate(pairs)]
    for copy in copies:
        copy.start()
    for copy in copies:
        copy.wait()
    own[(slices + 2) * rows : (slices + 3) * rows] = mask_in[...].astype(jnp.float32)
    own[top : top + lists] = cells_in[...].astype(jnp.float32)
    y = lax.axis_index("gy")
    lane = lane_of((rows, LANES))
    for i, send in enumerate(sends):
        first = jnp.where(reaches_after(y, i, sides), cols - HALO, 0)
        out = jnp.zeros((rows, LANES), jnp.float32)
        for j in range(slices + 4):
            shift = (HALO * j - first + 2 * LANES) % LANES
            moved = pltpu.roll(own[j * rows : (j + 1) * rows], shift, 1)
            out = jnp.where((lane >= HALO * j) & (lane < HALO * (j + 1)), moved, out)
        send[0:rows] = out
        send[rows : rows + 2 * lists] = own[top : top + 2 * lists]


def pack_kernel(dims, *refs):
    slices, rows, cols, lists, group, sides, cut, width = dims
    own = refs[0]
    near = refs[1 : 1 + sides]
    blocks = refs[1 + sides : 1 + sides + group]
    statics = refs[1 + sides + group]
    me = lax.axis_index("tm")
    y = lax.axis_index("gy")
    last_y = lax.axis_size("gy") - 1
    lane = lane_of((rows, LANES))
    top = (slices + 4) * rows

    def placed(number, start, offset):
        column = lane - offset + start
        shift = offset - start + 4 * LANES
        value = pltpu.roll(own[number * rows : (number + 1) * rows], shift % LANES, 1)
        for i, ref in enumerate(near):
            after = reaches_after(y, i, sides)
            there = pltpu.roll(ref[0:rows], (shift - HALO * number + jnp.where(after, cols, -HALO)) % LANES, 1)
            if sides == 1:
                beyond = (column < 0) | (column >= cols)
            else:
                beyond = ((column >= cols) & after) | ((column < 0) & jnp.logical_not(after))
            value = jnp.where(beyond, there, value)
        if number == slices + 2:
            left = (column < 0) & (y == 0)
            right = (column >= cols) & (y == last_y)
            value = jnp.where(left | right, 0.0, value)
        return value

    def packed(numbers, start):
        out = placed(numbers[0], start, 0)
        for s, number in enumerate(numbers[1:], 1):
            out = jnp.where(lane >= s * width, placed(number, start, s * width), out)
        return out

    for k in range(group):
        start = partner(me, k, group) * cut - HALO
        blocks[k][0:rows] = packed(list(range(slices)), start)
        blocks[k][rows : rows + 2 * lists] = own[top : top + 2 * lists]
        for i, ref in enumerate(near):
            low = rows + 2 * lists * (i + 1)
            blocks[k][low : low + 2 * lists] = ref[rows : rows + 2 * lists]
    start = me * cut - HALO
    statics[0] = packed([slices, slices + 1], start)
    statics[1] = packed([slices + 2, slices + 3], start)


def maps_kernel(dims, *refs):
    slices, rows, cols, lists, _, sides, cut, width = dims
    blocks, maps = refs[: len(refs) // 2], refs[len(refs) // 2 :]
    start = lax.axis_index("tm") * cut - HALO
    y = lax.axis_index("gy")
    each = lists // slices
    rounded = lambda v: v.astype(jnp.bfloat16)
    n = lists // slices * LANES * (1 + sides)
    narrow = lambda v: v.astype(jnp.int16)
    down = narrow(lax.broadcasted_iota(jnp.int32, (rows, n), 0))
    across = narrow(lax.broadcasted_iota(jnp.int32, (width, n), 0))

    def chosen(where, weight):
        weight = rounded(jnp.broadcast_to(weight, (1, n)))
        return jnp.where(where, jnp.broadcast_to(weight, where.shape), jnp.zeros(where.shape, jnp.bfloat16))

    for block, target in zip(blocks, maps):
        row, col, parts = [], [], []
        for side in range(1 + sides):
            low = rows + 2 * lists * side
            shift = -start
            if side:
                shift = shift + jnp.where(reaches_after(y, side - 1, sides), cols, -cols)
            cell = block[low : low + lists].astype(jnp.int32)
            value = block[low + lists : low + 2 * lists]
            part1 = rounded(value).astype(jnp.float32)
            part2 = rounded(value - part1).astype(jnp.float32)
            if cols & (cols - 1) == 0:
                row.append(cell >> (cols.bit_length() - 1))
                col.append((cell & (cols - 1)) + shift)
            else:
                row.append(cell // cols)
                col.append(cell % cols + shift)
            parts.append((part1, part2, value - part1 - part2))

        def line(arrays, s):
            return jnp.concatenate([v[j : j + 1] for v in arrays for j in range(s * each, (s + 1) * each)], axis=1)

        found = [[], []]
        for s in range(slices):
            at_row = down == narrow(line(row, s))
            at_col = across == narrow(line(col, s))
            left = chosen(at_row, 1.0)
            weights = [1.0] + [line([p[i] for p in parts], s) for i in range(3)]
            right = jnp.concatenate([chosen(at_col, w) for w in weights], axis=0)
            out = lax.dot_general(left, right, (((1,), (1,)), ((), ())), preferred_element_type=jnp.float32)
            found[0].append(out[:, 0:width])
            found[1].append(
                out[:, width : 2 * width] + (out[:, 2 * width : 3 * width] + out[:, 3 * width : 4 * width])
            )
        for i in range(2):
            pieces = found[i]
            if slices * width < LANES:
                pieces = pieces + [jnp.zeros((rows, LANES - slices * width), jnp.float32)]
            target[i] = jnp.concatenate(pieces, axis=1)


def edge_kernel(dims, *refs):
    rows, count, swaps = dims
    blocks, maps = refs[:count], refs[count : 2 * count]
    statics, sends = refs[2 * count : -swaps], refs[-swaps:]
    x = lax.axis_index("gx")
    for i, send in enumerate(sends):
        lower = reaches_after(x, i, swaps)
        low = pl.multiple_of(jnp.where(lower, rows - HALO, 0), 8)
        for k in range(count):
            base = k * (HALO + 2 * REACH)
            send[base : base + HALO] = blocks[k][pl.ds(low, HALO)]
            for j in range(2):
                first = base + HALO + j * REACH
                send[first : first + REACH] = jnp.where(lower, maps[k][j, rows - REACH : rows], maps[k][j, 0:REACH])
        for ref in statics:
            for j in range(2):
                first = count * (HALO + 2 * REACH) + j * HALO
                send[first : first + HALO] = ref[j, pl.ds(low, HALO)]


def main_kernel(dims, *refs):
    slices, rows, group, sides, cut, width = dims
    blocks, statics, maps = refs[:group], refs[group], refs[group + 1 : 2 * group + 1]
    refs = refs[2 * group + 1 :]
    early, late, outs = refs[:sides], refs[sides : 2 * sides], refs[2 * sides : 2 * sides + group]
    state, count, total, fixed, final, misfit, keep, coef, slide = refs[2 * sides + group :]
    me = lax.axis_index("tm")
    x = lax.axis_index("gx")
    last_x = lax.axis_size("gx") - 1
    full = rows + 2 * HALO
    wrap = (slices - 1) * width

    def put(target, main, pieces, reach):
        after = reaches_after(x, 0, sides) if sides else None
        zero = jnp.zeros((reach, LANES), jnp.float32)
        one, two = (list(pieces) + [zero, zero])[:2]
        if reach < HALO:
            target[0:8] = jnp.zeros((8, LANES), jnp.float32)
            target[full - 8 : full] = jnp.zeros((8, LANES), jnp.float32)
        target[HALO - reach : HALO] = jnp.where(after, two, one) if sides else zero
        target[HALO : HALO + rows] = main
        target[HALO + rows : HALO + rows + reach] = jnp.where(after, one, two) if sides else zero

    stride = HALO + 2 * REACH
    for k in range(group):
        pair = source(me, k, group)
        edges, base = (late, (k - 1) * stride) if k else (early, 0)
        put(state.at[pair], blocks[k][0:rows], [e[base : base + HALO] for e in edges], HALO)
        for j, target in enumerate((count, total)):
            first = base + HALO + j * REACH
            put(target.at[pair], maps[k][j], [e[first : first + REACH] for e in edges], REACH)
    for j in range(2):
        first = stride + j * HALO
        put(fixed.at[j], statics[j], [e[first : first + HALO] for e in early], HALO)

    row = lax.broadcasted_iota(jnp.int32, (full, LANES), 0)
    lane = lane_of((full, LANES))
    down = lambda v: pltpu.roll(v, v.shape[0] - 1, 0)
    up = lambda v: pltpu.roll(v, 1, 0)
    right = lambda v: pltpu.roll(v, LANES - 1, 1)
    left = lambda v: pltpu.roll(v, 1, 1)
    slide[:, :, 0:8] = jnp.zeros((2, group, 8, LANES), jnp.float32)
    slide[:, :, full + 8 : full + 16] = jnp.zeros((2, group, 8, LANES), jnp.float32)

    def spread(value):
        out = value
        for s in range(1, slices):
            out = jnp.where(lane[: value.shape[0]] >= s * width, pltpu.roll(value, s * width, 1), out)
        return out

    second = lambda v: pltpu.roll(v, LANES - width, 1)
    outside = ((row < HALO) & (x == 0)) | ((row >= HALO + rows) & (x == last_x))
    mask = jnp.where(outside, 0.0, spread(fixed[1]))
    rate = spread(second(fixed[1]))
    prior = spread(fixed[0])
    background = second(fixed[0])
    seam = lane % width == width - 1
    if LANES != slices * width:
        seam = seam | (lane >= slices * width)
    coef[0] = 0.25 * (rate + down(rate)) * (mask * down(mask))
    coef[1] = jnp.where(seam, 0.0, 0.25 * (rate + right(rate)) * (mask * right(mask)))
    fixed[0] = prior
    fixed[1] = background
    fixed[2] = prior

    pairs = range(group)
    for outer in range(OUTER):
        low = 2 * STEPS * outer
        high = full - low
        size = high - low
        span = pl.ds(low, size)
        here = lane[:size]

        def slid(number, values, by):
            for p in pairs:
                slide[number, p, 8 + low : 8 + high] = values[p]
            return [slide[number, p, 8 + low + by : 8 + high + by] for p in pairs]

        moves = (
            (lambda v: slid(0, v, 1), lambda v: slid(1, v, -1)),
            (lambda v: [right(w) for w in v], lambda v: [left(w) for w in v]),
        )
        bed = fixed[2, span]
        coef[0, span] = jnp.where(row[:size] == size - 1, 0.0, coef[0, span])
        coef[2, span] = down(bed) - bed
        coef[3, span] = right(bed) - bed

        thick = [state[p, span] for p in pairs]
        for step in range(STEPS):
            fluxes = []
            for d, (ahead, behind) in enumerate(moves):
                there = ahead(thick)
                flux = []
                for p in pairs:
                    both = thick[p] + there[p]
                    slope = (there[p] - thick[p]) + coef[2 + d, span]
                    scaled = coef[d, span] * both
                    half = 0.5 * both
                    by_mean = scaled * slope
                    keep[p, step, 2 * d, span] = half * scaled
                    keep[p, step, 2 * d + 1, span] = by_mean
                    flux.append(half * by_mean)
                fluxes.append((flux, behind(flux)))
            thick = [
                thick[p] + ((fluxes[0][0][p] - fluxes[0][1][p]) + (fluxes[1][0][p] - fluxes[1][1][p])) for p in pairs
            ]
        for p in pairs:
            final[p, span] = thick[p]

        for p in pairs:
            own = final[p, span]
            start = pltpu.roll(final[p - 1, span], (LANES - wrap) % LANES, 1) if p else fixed[1, span]
            earlier = jnp.where(here < width, start, pltpu.roll(own, width, 1))
            misfit[p, span] = state[p, span] - earlier
        pull = []
        for p in pairs:
            later = pltpu.roll(misfit[p, span], LANES - width, 1)
            after = pltpu.roll(misfit[p + 1, span], wrap, 1) if p + 1 < group else 0.0
            later = jnp.where(here < wrap, later, after)
            pull.append(count[p, span] * final[p, span] - total[p, span] - later)

        sums = [None, None]
        for step in reversed(range(STEPS)):
            parts = []
            for d, (ahead, behind) in enumerate(moves):
                jump = [v - w for v, w in zip(pull, ahead(pull))]
                own, passed = [], []
                for p in pairs:
                    by_slope = keep[p, step, 2 * d, span] * jump[p]
                    by_mean = keep[p, step, 2 * d + 1, span] * jump[p]
                    sums[d] = by_slope if sums[d] is None else sums[d] + by_slope
                    own.append(by_mean - by_slope)
                    passed.append(by_mean + by_slope)
                parts.append((own, behind(passed)))
            pull = [pull[p] + ((parts[0][0][p] + parts[0][1][p]) + (parts[1][0][p] + parts[1][1][p])) for p in pairs]
        for p in pairs:
            state[p, span] = state[p, span] - state_rate * (misfit[p, span] + pull[p])
        by_x, by_y = sums
        each = (up(by_x) - by_x) + (left(by_y) - by_y)
        summed = each
        for s in range(1, slices):
            summed = summed + pltpu.roll(each, LANES - s * width, 1)
        fixed[2, span] = bed - bed_rate * (spread(summed) + (bed - prior[low:high]))

    inner = slice(HALO, HALO + rows)

    def fold(value, used):
        parts = LANES // used
        height = value.shape[0] // parts
        out = value[0:height]
        place = lane_of((height, LANES))
        for i in range(1, parts):
            moved = pltpu.roll(value[i * height : (i + 1) * height], i * used, 1)
            out = jnp.where(place >= i * used, moved, out)
        return out

    place = lane_of((rows, LANES))
    ground = fold(pltpu.roll(fixed[2, inner], LANES - HALO, 1), cut)
    for k in range(group):
        mine = state[partner(me, k, group), inner]
        out = pltpu.roll(mine, LANES - HALO, 1)
        for s in range(1, slices):
            out = jnp.where(place >= s * cut, pltpu.roll(mine, (s * cut - s * width - HALO) % LANES, 1), out)
        folded = fold(out, slices * cut)
        outs[k][0 : folded.shape[0]] = folded
        outs[k][folded.shape[0] :] = ground


def join_kernel(dims, *refs):
    slices, rows, group, cut = dims
    pieces, states, bed = refs[:group], refs[group], refs[group + 1]
    me = lax.axis_index("tm")
    height = rows * slices * cut // LANES
    for target, used, low, count in [(states.at[s], slices * cut, s * cut, height) for s in range(slices)] + [
        (bed, cut, 0, rows * cut // LANES)
    ]:
        base = 0 if count == height and target is not bed else height
        lane = lane_of((count, LANES))
        for i in range(LANES // used):
            out = jnp.zeros((count, LANES), jnp.float32)
            for k in range(group):
                first = source(me, k, group) * cut
                moved = pltpu.roll(pieces[k][base : base + count], (first - i * used - low + 2 * LANES) % LANES, 1)
                out = jnp.where((lane >= first) & (lane < first + cut), moved, out)
            target[i * count : (i + 1) * count] = out


def step(states, bed, background_state, ice_mask, flow_rate, obs_cell, obs_value):
    slices, rows, cols = states.shape
    group = lax.axis_size("tm")
    cut = cols // group
    width = cut + 2 * HALO
    full = rows + 2 * HALO
    lists = slices * obs_cell.shape[-1] // LANES
    f32 = lambda *shape: jax.ShapeDtypeStruct(shape, jnp.float32)
    vmem = lambda *shape: pltpu.VMEM(shape, jnp.float32)

    swaps_y = neighbour_swaps("gy")
    sides = len(swaps_y)
    own, *sends = call(
        functools.partial(copy_kernel, (slices, rows, cols, lists, sides)),
        [f32((slices + 4) * rows + 2 * lists, cols)] + [f32(rows + 2 * lists, LANES)] * sides,
        [pltpu.with_memory_space_constraint(v, pltpu.HBM) for v in (states, bed, background_state, ice_mask, flow_rate, obs_cell.reshape(lists, LANES), obs_value.reshape(lists, LANES))],
        [pltpu.VMEM((rows, cols), jnp.int32), pltpu.VMEM((lists, LANES), jnp.int32), pltpu.SemaphoreType.DMA((slices + 6,))],
        inputs=pltpu.HBM,
    )
    near = swap_all(sends, "gy")
    dims = (slices, rows, cols, lists, group, sides, cut, width)
    *blocks, statics = call(
        functools.partial(pack_kernel, dims),
        [f32(rows + 2 * lists * (1 + sides), LANES)] * group + [f32(2, rows, LANES)],
        [own, *near],
    )
    blocks = exchange_all(blocks)
    maps = []
    for part in (blocks[:1], blocks[1:]):
        if part:
            maps += call(functools.partial(maps_kernel, dims), [f32(2, rows, LANES)] * len(part), part)
    early, late = [], []
    swaps = len(neighbour_swaps("gx"))
    stride = HALO + 2 * REACH
    if swaps:
        sends = call(
            functools.partial(edge_kernel, (rows, 1, swaps)),
            [f32(stride + 2 * HALO, LANES)] * swaps,
            [blocks[0], maps[0], statics],
        )
        early = swap_all(sends, "gx")
        late = early
        if group > 1:
            sends = call(
                functools.partial(edge_kernel, (rows, group - 1, swaps)),
                [f32((group - 1) * stride, LANES)] * swaps,
                [*blocks[1:], *maps[1:]],
            )
            late = swap_all(sends, "gx")
    packed = call(
        functools.partial(main_kernel, (slices, rows, group, swaps, cut, width)),
        [f32(rows * (slices + 1) * cut // LANES, LANES)] * group,
        [*blocks, statics, *maps, *early, *late],
        [vmem(group, full, LANES)] * 3
        + [vmem(3, full, LANES)]
        + [vmem(group, full, LANES)] * 2
        + [vmem(group, STEPS, 4, full, LANES), vmem(4, full, LANES), vmem(2, group, full + 16, LANES)],
    )
    pieces = exchange_all(packed)
    return tuple(
        call(
            functools.partial(join_kernel, (slices, rows, group, cut)),
            [f32(slices, rows, cols), f32(rows, cols)],
            pieces,
        )
    )


def solution(mesh):
    placed = (
        P("tm", "gx", "gy"),
        P("gx", "gy"),
        P("gx", "gy"),
        P("gx", "gy"),
        P("gx", "gy"),
        P("tm", "gx", "gy", None),
        P("tm", "gx", "gy", None),
    )
    return jax.shard_map(
        step,
        mesh=mesh,
        in_specs=placed,
        out_specs=(P("tm", "gx", "gy"), P("gx", "gy")),
        check_vma=False,
    )
```

```python
import functools

import jax
import jax.numpy as jnp
from jax import lax
from jax.experimental import pallas as pl
from jax.experimental.pallas import tpu as pltpu
from jax.sharding import PartitionSpec as P


STEPS = 4
OUTER = 2
HALO = 2 * STEPS * OUTER
REACH = HALO - STEPS
LANES = 128

bed_rate = 0.1
state_rate = 0.5


def partner(index, number, count):
    shift = (count - number) % count
    if count & (count - 1) == 0:
        return index ^ shift
    return (index + shift) % count


def source(index, number, count):
    shift = (count - number) % count
    if count & (count - 1) == 0:
        return index ^ shift
    return (index + count - shift) % count


def exchange(value, axis, number):
    count = lax.axis_size(axis)
    return lax.ppermute(value, axis, [(i, partner(i, number, count)) for i in range(count)])


def neighbour_swaps(axis):
    count = lax.axis_size(axis)
    if count == 1:
        return []
    near = [(i, i ^ 1) for i in range(count)]
    if count == 2:
        return [near]
    far = []
    for i in range(1, count, 2):
        j = (i + 1) % count
        far += [(i, j), (j, i)]
    return [far, near]


def reaches_after(index, number, swaps):
    return (index & 1) == (0 if number == swaps - 1 else 1)


def exchange_all(values):
    out = list(values)
    for k in range(1, len(values)):
        out[k] = exchange(values[k], "tm", k)
    return out


def swap_all(values, axis):
    out = []
    for value, pairs in zip(values, neighbour_swaps(axis)):
        out.append(lax.ppermute(value, axis, pairs))
    return out


def call(kernel, out_shape, operands, scratch=(), inputs=pltpu.VMEM):
    spec = pl.BlockSpec(memory_space=pltpu.VMEM)
    return pl.pallas_call(
        kernel,
        out_shape=out_shape,
        in_specs=[pl.BlockSpec(memory_space=inputs)] * len(operands),
        out_specs=jax.tree.map(lambda _: spec, out_shape),
        scratch_shapes=list(scratch),
        compiler_params=pltpu.CompilerParams(vmem_limit_bytes=16 << 20),
    )(*operands)


def lane_of(shape):
    return lax.broadcasted_iota(jnp.int32, shape, len(shape) - 1)


def copy_kernel(dims, *refs):
    slices, rows, cols, lists, sides = dims
    states, bed, back, mask, rate, cells, values = refs[:7]
    own = refs[7]
    sends = refs[8 : 8 + sides]
    mask_in, cells_in, sems = refs[8 + sides :]
    top = (slices + 4) * rows
    pairs = [(states.at[s], own.at[s * rows : (s + 1) * rows]) for s in range(slices)]
    for i, ref in ((0, bed), (1, back), (3, rate)):
        pairs.append((ref, own.at[(slices + i) * rows : (slices + i + 1) * rows]))
    pairs += [(mask, mask_in), (cells, cells_in), (values, own.at[top + lists : top + 2 * lists])]
    copies = [pltpu.make_async_copy(a, b, sems.at[i]) for i, (a, b) in enumerate(pairs)]
    for copy in copies:
        copy.start()
    for copy in copies:
        copy.wait()
    own[(slices + 2) * rows : (slices + 3) * rows] = mask_in[...].astype(jnp.float32)
    own[top : top + lists] = cells_in[...].astype(jnp.float32)
    y = lax.axis_index("gy")
    lane = lane_of((rows, LANES))
    for i, send in enumerate(sends):
        first = jnp.where(reaches_after(y, i, sides), cols - HALO, 0)
        out = jnp.zeros((rows, LANES), jnp.float32)
        for j in range(slices + 4):
            shift = (HALO * j - first + 2 * LANES) % LANES
            moved = pltpu.roll(own[j * rows : (j + 1) * rows], shift, 1)
            out = jnp.where((lane >= HALO * j) & (lane < HALO * (j + 1)), moved, out)
        send[0:rows] = out
        send[rows : rows + 2 * lists] = own[top : top + 2 * lists]


def pack_kernel(dims, *refs):
    slices, rows, cols, lists, group, sides, cut, width = dims
    own = refs[0]
    near = refs[1 : 1 + sides]
    blocks = refs[1 + sides : 1 + sides + group]
    statics = refs[1 + sides + group]
    me = lax.axis_index("tm")
    y = lax.axis_index("gy")
    last_y = lax.axis_size("gy") - 1
    lane = lane_of((rows, LANES))
    top = (slices + 4) * rows

    def placed(number, start, offset):
        column = lane - offset + start
        shift = offset - start + 4 * LANES
        value = pltpu.roll(own[number * rows : (number + 1) * rows], shift % LANES, 1)
        for i, ref in enumerate(near):
            after = reaches_after(y, i, sides)
            there = pltpu.roll(ref[0:rows], (shift - HALO * number + jnp.where(after, cols, -HALO)) % LANES, 1)
            if sides == 1:
                beyond = (column < 0) | (column >= cols)
            else:
                beyond = ((column >= cols) & after) | ((column < 0) & jnp.logical_not(after))
            value = jnp.where(beyond, there, value)
        if number == slices + 2:
            left = (column < 0) & (y == 0)
            right = (column >= cols) & (y == last_y)
            value = jnp.where(left | right, 0.0, value)
        return value

    def packed(numbers, start):
        out = placed(numbers[0], start, 0)
        for s, number in enumerate(numbers[1:], 1):
            out = jnp.where(lane >= s * width, placed(number, start, s * width), out)
        return out

    for k in range(group):
        start = partner(me, k, group) * cut - HALO
        blocks[k][0:rows] = packed(list(range(slices)), start)
        blocks[k][rows : rows + 2 * lists] = own[top : top + 2 * lists]
        for i, ref in enumerate(near):
            low = rows + 2 * lists * (i + 1)
            blocks[k][low : low + 2 * lists] = ref[rows : rows + 2 * lists]
    start = me * cut - HALO
    statics[0] = packed([slices, slices + 1], start)
    statics[1] = packed([slices + 2, slices + 3], start)


def maps_kernel(dims, *refs):
    slices, rows, cols, lists, _, sides, cut, width = dims
    blocks, maps = refs[: len(refs) // 2], refs[len(refs) // 2 :]
    start = lax.axis_index("tm") * cut - HALO
    y = lax.axis_index("gy")
    each = lists // slices
    rounded = lambda v: v.astype(jnp.bfloat16)
    n = lists // slices * LANES * (1 + sides)
    narrow = lambda v: v.astype(jnp.int16)
    down = narrow(lax.broadcasted_iota(jnp.int32, (rows, n), 0))
    across = narrow(lax.broadcasted_iota(jnp.int32, (width, n), 0))

    def chosen(where, weight):
        weight = rounded(jnp.broadcast_to(weight, (1, n)))
        return jnp.where(where, jnp.broadcast_to(weight, where.shape), jnp.zeros(where.shape, jnp.bfloat16))

    for block, target in zip(blocks, maps):
        row, col, parts = [], [], []
        for side in range(1 + sides):
            low = rows + 2 * lists * side
            shift = -start
            if side:
                shift = shift + jnp.where(reaches_after(y, side - 1, sides), cols, -cols)
            cell = block[low : low + lists].astype(jnp.int32)
            value = block[low + lists : low + 2 * lists]
            part1 = rounded(value).astype(jnp.float32)
            part2 = rounded(value - part1).astype(jnp.float32)
            if cols & (cols - 1) == 0:
                row.append(cell >> (cols.bit_length() - 1))
                col.append((cell & (cols - 1)) + shift)
            else:
                row.append(cell // cols)
                col.append(cell % cols + shift)
            parts.append((part1, part2))

        def line(arrays, s):
            return jnp.concatenate([v[j : j + 1] for v in arrays for j in range(s * each, (s + 1) * each)], axis=1)

        found = [[], []]
        for s in range(slices):
            at_row = down == narrow(line(row, s))
            at_col = across == narrow(line(col, s))
            left = chosen(at_row, 1.0)
            weights = [1.0] + [line([p[i] for p in parts], s) for i in range(2)]
            right = jnp.concatenate([chosen(at_col, w) for w in weights], axis=0)
            out = lax.dot_general(left, right, (((1,), (1,)), ((), ())), preferred_element_type=jnp.float32)
            found[0].append(out[:, 0:width])
            found[1].append(out[:, width : 2 * width] + out[:, 2 * width : 3 * width])
        for i in range(2):
            pieces = found[i]
            if slices * width < LANES:
                pieces = pieces + [jnp.zeros((rows, LANES - slices * width), jnp.float32)]
            target[i] = jnp.concatenate(pieces, axis=1)


def edge_kernel(dims, *refs):
    rows, count, swaps = dims
    blocks, maps = refs[:count], refs[count : 2 * count]
    statics, sends = refs[2 * count : -swaps], refs[-swaps:]
    x = lax.axis_index("gx")
    for i, send in enumerate(sends):
        lower = reaches_after(x, i, swaps)
        low = pl.multiple_of(jnp.where(lower, rows - HALO, 0), 8)
        for k in range(count):
            base = k * (HALO + 2 * REACH)
            send[base : base + HALO] = blocks[k][pl.ds(low, HALO)]
            for j in range(2):
                first = base + HALO + j * REACH
                send[first : first + REACH] = jnp.where(lower, maps[k][j, rows - REACH : rows], maps[k][j, 0:REACH])
        for ref in statics:
            for j in range(2):
                first = count * (HALO + 2 * REACH) + j * HALO
                send[first : first + HALO] = ref[j, pl.ds(low, HALO)]


def main_kernel(dims, *refs):
    slices, rows, group, sides, cut, width = dims
    blocks, statics, maps = refs[:group], refs[group], refs[group + 1 : 2 * group + 1]
    refs = refs[2 * group + 1 :]
    early, late, outs = refs[:sides], refs[sides : 2 * sides], refs[2 * sides : 2 * sides + group]
    state, count, total, fixed, final, misfit, keep, coef, slide = refs[2 * sides + group :]
    me = lax.axis_index("tm")
    x = lax.axis_index("gx")
    last_x = lax.axis_size("gx") - 1
    full = rows + 2 * HALO
    wrap = (slices - 1) * width

    def put(target, main, pieces, reach):
        after = reaches_after(x, 0, sides) if sides else None
        zero = jnp.zeros((reach, LANES), jnp.float32)
        one, two = (list(pieces) + [zero, zero])[:2]
        if reach < HALO:
            target[0:8] = jnp.zeros((8, LANES), jnp.float32)
            target[full - 8 : full] = jnp.zeros((8, LANES), jnp.float32)
        target[HALO - reach : HALO] = jnp.where(after, two, one) if sides else zero
        target[HALO : HALO + rows] = main
        target[HALO + rows : HALO + rows + reach] = jnp.where(after, one, two) if sides else zero

    stride = HALO + 2 * REACH
    for k in range(group):
        pair = source(me, k, group)
        edges, base = (late, (k - 1) * stride) if k else (early, 0)
        put(state.at[pair], blocks[k][0:rows], [e[base : base + HALO] for e in edges], HALO)
        for j, target in enumerate((count, total)):
            first = base + HALO + j * REACH
            put(target.at[pair], maps[k][j], [e[first : first + REACH] for e in edges], REACH)
    for j in range(2):
        first = stride + j * HALO
        put(fixed.at[j], statics[j], [e[first : first + HALO] for e in early], HALO)

    row = lax.broadcasted_iota(jnp.int32, (full, LANES), 0)
    lane = lane_of((full, LANES))
    down = lambda v: pltpu.roll(v, v.shape[0] - 1, 0)
    up = lambda v: pltpu.roll(v, 1, 0)
    right = lambda v: pltpu.roll(v, LANES - 1, 1)
    left = lambda v: pltpu.roll(v, 1, 1)
    slide[:, :, 0:8] = jnp.zeros((2, group, 8, LANES), jnp.float32)
    slide[:, :, full + 8 : full + 16] = jnp.zeros((2, group, 8, LANES), jnp.float32)

    def spread(value):
        out = value
        for s in range(1, slices):
            out = jnp.where(lane[: value.shape[0]] >= s * width, pltpu.roll(value, s * width, 1), out)
        return out

    second = lambda v: pltpu.roll(v, LANES - width, 1)
    outside = ((row < HALO) & (x == 0)) | ((row >= HALO + rows) & (x == last_x))
    mask = jnp.where(outside, 0.0, spread(fixed[1]))
    rate = spread(second(fixed[1]))
    prior = spread(fixed[0])
    background = second(fixed[0])
    seam = lane % width == width - 1
    if LANES != slices * width:
        seam = seam | (lane >= slices * width)
    coef[0] = 0.25 * (rate + down(rate)) * (mask * down(mask))
    coef[1] = jnp.where(seam, 0.0, 0.25 * (rate + right(rate)) * (mask * right(mask)))
    fixed[0] = prior
    fixed[1] = background
    fixed[2] = prior

    pairs = range(group)
    for outer in range(OUTER):
        low = 2 * STEPS * outer
        high = full - low
        size = high - low
        span = pl.ds(low, size)
        here = lane[:size]

        def slid(number, values, by):
            for p in pairs:
                slide[number, p, 8 + low : 8 + high] = values[p]
            return [slide[number, p, 8 + low + by : 8 + high + by] for p in pairs]

        moves = (
            (lambda v: slid(0, v, 1), lambda v: slid(1, v, -1)),
            (lambda v: [right(w) for w in v], lambda v: [left(w) for w in v]),
        )
        bed = fixed[2, span]
        coef[0, span] = jnp.where(row[:size] == size - 1, 0.0, coef[0, span])
        coef[2, span] = down(bed) - bed
        coef[3, span] = right(bed) - bed

        thick = [state[p, span] for p in pairs]
        for step in range(STEPS):
            fluxes = []
            for d, (ahead, behind) in enumerate(moves):
                there = ahead(thick)
                flux = []
                for p in pairs:
                    both = thick[p] + there[p]
                    slope = (there[p] - thick[p]) + coef[2 + d, span]
                    scaled = coef[d, span] * both
                    half = 0.5 * both
                    by_mean = scaled * slope
                    keep[p, step, 2 * d, span] = half * scaled
                    keep[p, step, 2 * d + 1, span] = by_mean
                    flux.append(half * by_mean)
                fluxes.append((flux, behind(flux)))
            thick = [
                thick[p] + ((fluxes[0][0][p] - fluxes[0][1][p]) + (fluxes[1][0][p] - fluxes[1][1][p])) for p in pairs
            ]
        for p in pairs:
            final[p, span] = thick[p]

        for p in pairs:
            own = final[p, span]
            start = pltpu.roll(final[p - 1, span], (LANES - wrap) % LANES, 1) if p else fixed[1, span]
            earlier = jnp.where(here < width, start, pltpu.roll(own, width, 1))
            misfit[p, span] = state[p, span] - earlier
        pull = []
        for p in pairs:
            later = pltpu.roll(misfit[p, span], LANES - width, 1)
            after = pltpu.roll(misfit[p + 1, span], wrap, 1) if p + 1 < group else 0.0
            later = jnp.where(here < wrap, later, after)
            pull.append(count[p, span] * final[p, span] - total[p, span] - later)

        sums = [None, None]
        for step in reversed(range(STEPS)):
            parts = []
            for d, (ahead, behind) in enumerate(moves):
                jump = [v - w for v, w in zip(pull, ahead(pull))]
                own, passed = [], []
                for p in pairs:
                    by_slope = keep[p, step, 2 * d, span] * jump[p]
                    by_mean = keep[p, step, 2 * d + 1, span] * jump[p]
                    sums[d] = by_slope if sums[d] is None else sums[d] + by_slope
                    own.append(by_mean - by_slope)
                    passed.append(by_mean + by_slope)
                parts.append((own, behind(passed)))
            pull = [pull[p] + ((parts[0][0][p] + parts[0][1][p]) + (parts[1][0][p] + parts[1][1][p])) for p in pairs]
        for p in pairs:
            state[p, span] = state[p, span] - state_rate * (misfit[p, span] + pull[p])
        by_x, by_y = sums
        each = (up(by_x) - by_x) + (left(by_y) - by_y)
        summed = each
        for s in range(1, slices):
            summed = summed + pltpu.roll(each, LANES - s * width, 1)
        fixed[2, span] = bed - bed_rate * (spread(summed) + (bed - prior[low:high]))

    inner = slice(HALO, HALO + rows)

    def fold(value, used):
        parts = LANES // used
        height = value.shape[0] // parts
        out = value[0:height]
        place = lane_of((height, LANES))
        for i in range(1, parts):
            moved = pltpu.roll(value[i * height : (i + 1) * height], i * used, 1)
            out = jnp.where(place >= i * used, moved, out)
        return out

    place = lane_of((rows, LANES))
    ground = fold(pltpu.roll(fixed[2, inner], LANES - HALO, 1), cut)
    for k in range(group):
        mine = state[partner(me, k, group), inner]
        out = pltpu.roll(mine, LANES - HALO, 1)
        for s in range(1, slices):
            out = jnp.where(place >= s * cut, pltpu.roll(mine, (s * cut - s * width - HALO) % LANES, 1), out)
        folded = fold(out, slices * cut)
        outs[k][0 : folded.shape[0]] = folded
        outs[k][folded.shape[0] :] = ground


def join_kernel(dims, *refs):
    slices, rows, group, cut = dims
    pieces, states, bed = refs[:group], refs[group], refs[group + 1]
    me = lax.axis_index("tm")
    height = rows * slices * cut // LANES
    for target, used, low, count in [(states.at[s], slices * cut, s * cut, height) for s in range(slices)] + [
        (bed, cut, 0, rows * cut // LANES)
    ]:
        base = 0 if count == height and target is not bed else height
        lane = lane_of((count, LANES))
        for i in range(LANES // used):
            out = jnp.zeros((count, LANES), jnp.float32)
            for k in range(group):
                first = source(me, k, group) * cut
                moved = pltpu.roll(pieces[k][base : base + count], (first - i * used - low + 2 * LANES) % LANES, 1)
                out = jnp.where((lane >= first) & (lane < first + cut), moved, out)
            target[i * count : (i + 1) * count] = out


def step(states, bed, background_state, ice_mask, flow_rate, obs_cell, obs_value):
    slices, rows, cols = states.shape
    group = lax.axis_size("tm")
    cut = cols // group
    width = cut + 2 * HALO
    full = rows + 2 * HALO
    lists = slices * obs_cell.shape[-1] // LANES
    f32 = lambda *shape: jax.ShapeDtypeStruct(shape, jnp.float32)
    vmem = lambda *shape: pltpu.VMEM(shape, jnp.float32)

    swaps_y = neighbour_swaps("gy")
    sides = len(swaps_y)
    own, *sends = call(
        functools.partial(copy_kernel, (slices, rows, cols, lists, sides)),
        [f32((slices + 4) * rows + 2 * lists, cols)] + [f32(rows + 2 * lists, LANES)] * sides,
        [pltpu.with_memory_space_constraint(v, pltpu.HBM) for v in (states, bed, background_state, ice_mask, flow_rate, obs_cell.reshape(lists, LANES), obs_value.reshape(lists, LANES))],
        [pltpu.VMEM((rows, cols), jnp.int32), pltpu.VMEM((lists, LANES), jnp.int32), pltpu.SemaphoreType.DMA((slices + 6,))],
        inputs=pltpu.HBM,
    )
    near = swap_all(sends, "gy")
    dims = (slices, rows, cols, lists, group, sides, cut, width)
    *blocks, statics = call(
        functools.partial(pack_kernel, dims),
        [f32(rows + 2 * lists * (1 + sides), LANES)] * group + [f32(2, rows, LANES)],
        [own, *near],
    )
    blocks = exchange_all(blocks)
    maps = []
    for part in (blocks[:1], blocks[1:]):
        if part:
            maps += call(functools.partial(maps_kernel, dims), [f32(2, rows, LANES)] * len(part), part)
    early, late = [], []
    swaps = len(neighbour_swaps("gx"))
    stride = HALO + 2 * REACH
    if swaps:
        sends = call(
            functools.partial(edge_kernel, (rows, 1, swaps)),
            [f32(stride + 2 * HALO, LANES)] * swaps,
            [blocks[0], maps[0], statics],
        )
        early = swap_all(sends, "gx")
        late = early
        if group > 1:
            sends = call(
                functools.partial(edge_kernel, (rows, group - 1, swaps)),
                [f32((group - 1) * stride, LANES)] * swaps,
                [*blocks[1:], *maps[1:]],
            )
            late = swap_all(sends, "gx")
    packed = call(
        functools.partial(main_kernel, (slices, rows, group, swaps, cut, width)),
        [f32(rows * (slices + 1) * cut // LANES, LANES)] * group,
        [*blocks, statics, *maps, *early, *late],
        [vmem(group, full, LANES)] * 3
        + [vmem(3, full, LANES)]
        + [vmem(group, full, LANES)] * 2
        + [vmem(group, STEPS, 4, full, LANES), vmem(4, full, LANES), vmem(2, group, full + 16, LANES)],
    )
    pieces = exchange_all(packed)
    return tuple(
        call(
            functools.partial(join_kernel, (slices, rows, group, cut)),
            [f32(slices, rows, cols), f32(rows, cols)],
            pieces,
        )
    )


def solution(mesh):
    placed = (
        P("tm", "gx", "gy"),
        P("gx", "gy"),
        P("gx", "gy"),
        P("gx", "gy"),
        P("gx", "gy"),
        P("tm", "gx", "gy", None),
        P("tm", "gx", "gy", None),
    )
    return jax.shard_map(
        step,
        mesh=mesh,
        in_specs=placed,
        out_specs=(P("tm", "gx", "gy"), P("gx", "gy")),
        check_vma=False,
    )
```

```python
import functools

import jax
import jax.numpy as jnp
from jax import lax
from jax.experimental import pallas as pl
from jax.experimental.pallas import tpu as pltpu
from jax.sharding import PartitionSpec as P


STEPS = 4
OUTER = 2
HALO = 2 * STEPS * OUTER
REACH = HALO - STEPS
LANES = 128

bed_rate = 0.1
state_rate = 0.5


def partner(index, number, count):
    shift = (count - number) % count
    if count & (count - 1) == 0:
        return index ^ shift
    return (index + shift) % count


def source(index, number, count):
    shift = (count - number) % count
    if count & (count - 1) == 0:
        return index ^ shift
    return (index + count - shift) % count


def exchange(value, axis, number):
    count = lax.axis_size(axis)
    return lax.ppermute(value, axis, [(i, partner(i, number, count)) for i in range(count)])


def neighbour_swaps(axis):
    count = lax.axis_size(axis)
    if count == 1:
        return []
    near = [(i, i ^ 1) for i in range(count)]
    if count == 2:
        return [near]
    far = []
    for i in range(1, count, 2):
        j = (i + 1) % count
        far += [(i, j), (j, i)]
    return [far, near]


def reaches_after(index, number, swaps):
    return (index & 1) == (0 if number == swaps - 1 else 1)


def exchange_all(values):
    out = list(values)
    for k in range(1, len(values)):
        out[k] = exchange(values[k], "tm", k)
    return out


def swap_all(values, axis):
    out = []
    for value, pairs in zip(values, neighbour_swaps(axis)):
        out.append(lax.ppermute(value, axis, pairs))
    return out


def call(kernel, out_shape, operands, scratch=(), inputs=pltpu.VMEM):
    spec = pl.BlockSpec(memory_space=pltpu.VMEM)
    return pl.pallas_call(
        kernel,
        out_shape=out_shape,
        in_specs=[pl.BlockSpec(memory_space=inputs)] * len(operands),
        out_specs=jax.tree.map(lambda _: spec, out_shape),
        scratch_shapes=list(scratch),
        compiler_params=pltpu.CompilerParams(vmem_limit_bytes=16 << 20),
    )(*operands)


def lane_of(shape):
    return lax.broadcasted_iota(jnp.int32, shape, len(shape) - 1)


def copy_kernel(dims, *refs):
    slices, rows, cols, lists, sides = dims
    states, bed, back, mask, rate, cells, values = refs[:7]
    own = refs[7]
    sends = refs[8 : 8 + sides]
    mask_in, cells_in, sems = refs[8 + sides :]
    top = (slices + 4) * rows
    pairs = [(states.at[s], own.at[s * rows : (s + 1) * rows]) for s in range(slices)]
    for i, ref in ((0, bed), (1, back), (3, rate)):
        pairs.append((ref, own.at[(slices + i) * rows : (slices + i + 1) * rows]))
    pairs += [(mask, mask_in), (cells, cells_in), (values, own.at[top + lists : top + 2 * lists])]
    copies = [pltpu.make_async_copy(a, b, sems.at[i]) for i, (a, b) in enumerate(pairs)]
    for copy in copies:
        copy.start()
    for copy in copies:
        copy.wait()
    own[(slices + 2) * rows : (slices + 3) * rows] = mask_in[...].astype(jnp.float32)
    own[top : top + lists] = cells_in[...].astype(jnp.float32)
    y = lax.axis_index("gy")
    lane = lane_of((rows, LANES))
    for i, send in enumerate(sends):
        first = jnp.where(reaches_after(y, i, sides), cols - HALO, 0)
        out = jnp.zeros((rows, LANES), jnp.float32)
        for j in range(slices + 4):
            shift = (HALO * j - first + 2 * LANES) % LANES
            moved = pltpu.roll(own[j * rows : (j + 1) * rows], shift, 1)
            out = jnp.where((lane >= HALO * j) & (lane < HALO * (j + 1)), moved, out)
        send[0:rows] = out
        send[rows : rows + 2 * lists] = own[top : top + 2 * lists]


def pack_kernel(dims, *refs):
    slices, rows, cols, lists, group, sides, cut, width, numbers = dims
    own = refs[0]
    near = refs[1 : 1 + sides]
    blocks = dict(zip(numbers, refs[1 + sides :]))
    me = lax.axis_index("tm")
    y = lax.axis_index("gy")
    last_y = lax.axis_size("gy") - 1
    lane = lane_of((rows, LANES))
    top = (slices + 4) * rows

    def placed(number, start, offset):
        column = lane - offset + start
        shift = offset - start + 4 * LANES
        value = pltpu.roll(own[number * rows : (number + 1) * rows], shift % LANES, 1)
        for i, ref in enumerate(near):
            after = reaches_after(y, i, sides)
            there = pltpu.roll(ref[0:rows], (shift - HALO * number + jnp.where(after, cols, -HALO)) % LANES, 1)
            if sides == 1:
                beyond = (column < 0) | (column >= cols)
            else:
                beyond = ((column >= cols) & after) | ((column < 0) & jnp.logical_not(after))
            value = jnp.where(beyond, there, value)
        if number == slices + 2:
            left = (column < 0) & (y == 0)
            right = (column >= cols) & (y == last_y)
            value = jnp.where(left | right, 0.0, value)
        return value

    def packed(numbers, start):
        out = placed(numbers[0], start, 0)
        for s, number in enumerate(numbers[1:], 1):
            out = jnp.where(lane >= s * width, placed(number, start, s * width), out)
        return out

    for k in numbers:
        start = partner(me, k, group) * cut - HALO
        blocks[k][0:rows] = packed(list(range(slices)), start)
        blocks[k][rows : rows + 2 * lists] = own[top : top + 2 * lists]
        for i, ref in enumerate(near):
            low = rows + 2 * lists * (i + 1)
            blocks[k][low : low + 2 * lists] = ref[rows : rows + 2 * lists]
    if 0 not in numbers:
        return
    statics = refs[-1]
    start = me * cut - HALO
    statics[0] = packed([slices, slices + 1], start)
    statics[1] = packed([slices + 2, slices + 3], start)


def maps_kernel(dims, *refs):
    slices, rows, cols, lists, _, sides, cut, width = dims
    blocks, maps = refs[: len(refs) // 2], refs[len(refs) // 2 :]
    start = lax.axis_index("tm") * cut - HALO
    y = lax.axis_index("gy")
    each = lists // slices
    rounded = lambda v: v.astype(jnp.bfloat16)
    n = lists // slices * LANES * (1 + sides)
    narrow = lambda v: v.astype(jnp.int16)
    down = narrow(lax.broadcasted_iota(jnp.int32, (rows, n), 0))
    across = narrow(lax.broadcasted_iota(jnp.int32, (width, n), 0))

    def chosen(where, weight):
        weight = rounded(jnp.broadcast_to(weight, (1, n)))
        return jnp.where(where, jnp.broadcast_to(weight, where.shape), jnp.zeros(where.shape, jnp.bfloat16))

    for block, target in zip(blocks, maps):
        row, col, parts = [], [], []
        for side in range(1 + sides):
            low = rows + 2 * lists * side
            shift = -start
            if side:
                shift = shift + jnp.where(reaches_after(y, side - 1, sides), cols, -cols)
            cell = block[low : low + lists].astype(jnp.int32)
            value = block[low + lists : low + 2 * lists]
            part1 = rounded(value).astype(jnp.float32)
            part2 = rounded(value - part1).astype(jnp.float32)
            if cols & (cols - 1) == 0:
                row.append(cell >> (cols.bit_length() - 1))
                col.append((cell & (cols - 1)) + shift)
            else:
                row.append(cell // cols)
                col.append(cell % cols + shift)
            parts.append((part1, part2))

        def line(arrays, s):
            return jnp.concatenate([v[j : j + 1] for v in arrays for j in range(s * each, (s + 1) * each)], axis=1)

        found = [[], []]
        for s in range(slices):
            at_row = down == narrow(line(row, s))
            at_col = across == narrow(line(col, s))
            left = chosen(at_row, 1.0)
            weights = [1.0] + [line([p[i] for p in parts], s) for i in range(2)]
            right = jnp.concatenate([chosen(at_col, w) for w in weights], axis=0)
            out = lax.dot_general(left, right, (((1,), (1,)), ((), ())), preferred_element_type=jnp.float32)
            found[0].append(out[:, 0:width])
            found[1].append(out[:, width : 2 * width] + out[:, 2 * width : 3 * width])
        for i in range(2):
            pieces = found[i]
            if slices * width < LANES:
                pieces = pieces + [jnp.zeros((rows, LANES - slices * width), jnp.float32)]
            target[i] = jnp.concatenate(pieces, axis=1)


def edge_kernel(dims, *refs):
    rows, count, swaps = dims
    blocks, maps = refs[:count], refs[count : 2 * count]
    statics, sends = refs[2 * count : -swaps], refs[-swaps:]
    x = lax.axis_index("gx")
    for i, send in enumerate(sends):
        lower = reaches_after(x, i, swaps)
        low = pl.multiple_of(jnp.where(lower, rows - HALO, 0), 8)
        for k in range(count):
            base = k * (HALO + 2 * REACH)
            send[base : base + HALO] = blocks[k][pl.ds(low, HALO)]
            for j in range(2):
                first = base + HALO + j * REACH
                send[first : first + REACH] = jnp.where(lower, maps[k][j, rows - REACH : rows], maps[k][j, 0:REACH])
        for ref in statics:
            for j in range(2):
                first = count * (HALO + 2 * REACH) + j * HALO
                send[first : first + HALO] = ref[j, pl.ds(low, HALO)]


def main_kernel(dims, *refs):
    slices, rows, group, sides, cut, width = dims
    blocks, statics, maps = refs[:group], refs[group], refs[group + 1 : 2 * group + 1]
    refs = refs[2 * group + 1 :]
    early, late, outs = refs[:sides], refs[sides : 2 * sides], refs[2 * sides : 2 * sides + group]
    state, count, total, fixed, final, misfit, keep, coef, slide = refs[2 * sides + group :]
    me = lax.axis_index("tm")
    x = lax.axis_index("gx")
    last_x = lax.axis_size("gx") - 1
    full = rows + 2 * HALO
    wrap = (slices - 1) * width

    def put(target, main, pieces, reach):
        after = reaches_after(x, 0, sides) if sides else None
        zero = jnp.zeros((reach, LANES), jnp.float32)
        one, two = (list(pieces) + [zero, zero])[:2]
        if reach < HALO:
            target[0:8] = jnp.zeros((8, LANES), jnp.float32)
            target[full - 8 : full] = jnp.zeros((8, LANES), jnp.float32)
        target[HALO - reach : HALO] = jnp.where(after, two, one) if sides else zero
        target[HALO : HALO + rows] = main
        target[HALO + rows : HALO + rows + reach] = jnp.where(after, one, two) if sides else zero

    stride = HALO + 2 * REACH
    for k in range(group):
        pair = source(me, k, group)
        edges, base = (late, (k - 1) * stride) if k else (early, 0)
        put(state.at[pair], blocks[k][0:rows], [e[base : base + HALO] for e in edges], HALO)
        for j, target in enumerate((count, total)):
            first = base + HALO + j * REACH
            put(target.at[pair], maps[k][j], [e[first : first + REACH] for e in edges], REACH)
    for j in range(2):
        first = stride + j * HALO
        put(fixed.at[j], statics[j], [e[first : first + HALO] for e in early], HALO)

    row = lax.broadcasted_iota(jnp.int32, (full, LANES), 0)
    lane = lane_of((full, LANES))
    down = lambda v: pltpu.roll(v, v.shape[0] - 1, 0)
    up = lambda v: pltpu.roll(v, 1, 0)
    right = lambda v: pltpu.roll(v, LANES - 1, 1)
    left = lambda v: pltpu.roll(v, 1, 1)
    slide[:, :, 0:8] = jnp.zeros((2, group, 8, LANES), jnp.float32)
    slide[:, :, full + 8 : full + 16] = jnp.zeros((2, group, 8, LANES), jnp.float32)

    def spread(value):
        out = value
        for s in range(1, slices):
            out = jnp.where(lane[: value.shape[0]] >= s * width, pltpu.roll(value, s * width, 1), out)
        return out

    second = lambda v: pltpu.roll(v, LANES - width, 1)
    outside = ((row < HALO) & (x == 0)) | ((row >= HALO + rows) & (x == last_x))
    mask = jnp.where(outside, 0.0, spread(fixed[1]))
    rate = spread(second(fixed[1]))
    prior = spread(fixed[0])
    background = second(fixed[0])
    seam = lane % width == width - 1
    if LANES != slices * width:
        seam = seam | (lane >= slices * width)
    coef[0] = 0.25 * (rate + down(rate)) * (mask * down(mask))
    coef[1] = jnp.where(seam, 0.0, 0.25 * (rate + right(rate)) * (mask * right(mask)))
    fixed[0] = prior
    fixed[1] = background
    fixed[2] = prior

    pairs = range(group)
    for outer in range(OUTER):
        low = 2 * STEPS * outer
        high = full - low
        size = high - low
        span = pl.ds(low, size)
        here = lane[:size]

        def slid(number, values, by):
            for p in pairs:
                slide[number, p, 8 + low : 8 + high] = values[p]
            return [slide[number, p, 8 + low + by : 8 + high + by] for p in pairs]

        moves = (
            (lambda v: slid(0, v, 1), lambda v: slid(1, v, -1)),
            (lambda v: [right(w) for w in v], lambda v: [left(w) for w in v]),
        )
        bed = fixed[2, span]
        coef[0, span] = jnp.where(row[:size] == size - 1, 0.0, coef[0, span])
        coef[2, span] = down(bed) - bed
        coef[3, span] = right(bed) - bed

        thick = [state[p, span] for p in pairs]
        for step in range(STEPS):
            fluxes = []
            for d, (ahead, behind) in enumerate(moves):
                there = ahead(thick)
                flux = []
                for p in pairs:
                    both = thick[p] + there[p]
                    slope = (there[p] - thick[p]) + coef[2 + d, span]
                    scaled = coef[d, span] * both
                    half = 0.5 * both
                    by_mean = scaled * slope
                    keep[p, step, 2 * d, span] = half * scaled
                    keep[p, step, 2 * d + 1, span] = by_mean
                    flux.append(half * by_mean)
                fluxes.append((flux, behind(flux)))
            thick = [
                thick[p] + ((fluxes[0][0][p] - fluxes[0][1][p]) + (fluxes[1][0][p] - fluxes[1][1][p])) for p in pairs
            ]
        for p in pairs:
            final[p, span] = thick[p]

        for p in pairs:
            own = final[p, span]
            start = pltpu.roll(final[p - 1, span], (LANES - wrap) % LANES, 1) if p else fixed[1, span]
            earlier = jnp.where(here < width, start, pltpu.roll(own, width, 1))
            misfit[p, span] = state[p, span] - earlier
        pull = []
        for p in pairs:
            later = pltpu.roll(misfit[p, span], LANES - width, 1)
            after = pltpu.roll(misfit[p + 1, span], wrap, 1) if p + 1 < group else 0.0
            later = jnp.where(here < wrap, later, after)
            pull.append(count[p, span] * final[p, span] - total[p, span] - later)

        sums = [None, None]
        for step in reversed(range(STEPS)):
            parts = []
            for d, (ahead, behind) in enumerate(moves):
                jump = [v - w for v, w in zip(pull, ahead(pull))]
                own, passed = [], []
                for p in pairs:
                    by_slope = keep[p, step, 2 * d, span] * jump[p]
                    by_mean = keep[p, step, 2 * d + 1, span] * jump[p]
                    sums[d] = by_slope if sums[d] is None else sums[d] + by_slope
                    own.append(by_mean - by_slope)
                    passed.append(by_mean + by_slope)
                parts.append((own, behind(passed)))
            pull = [pull[p] + ((parts[0][0][p] + parts[0][1][p]) + (parts[1][0][p] + parts[1][1][p])) for p in pairs]
        for p in pairs:
            state[p, span] = state[p, span] - state_rate * (misfit[p, span] + pull[p])
        by_x, by_y = sums
        each = (up(by_x) - by_x) + (left(by_y) - by_y)
        summed = each
        for s in range(1, slices):
            summed = summed + pltpu.roll(each, LANES - s * width, 1)
        fixed[2, span] = bed - bed_rate * (spread(summed) + (bed - prior[low:high]))

    inner = slice(HALO, HALO + rows)

    def fold(value, used):
        parts = LANES // used
        height = value.shape[0] // parts
        out = value[0:height]
        place = lane_of((height, LANES))
        for i in range(1, parts):
            moved = pltpu.roll(value[i * height : (i + 1) * height], i * used, 1)
            out = jnp.where(place >= i * used, moved, out)
        return out

    place = lane_of((rows, LANES))
    ground = fold(pltpu.roll(fixed[2, inner], LANES - HALO, 1), cut)
    for k in range(group):
        mine = state[partner(me, k, group), inner]
        out = pltpu.roll(mine, LANES - HALO, 1)
        for s in range(1, slices):
            out = jnp.where(place >= s * cut, pltpu.roll(mine, (s * cut - s * width - HALO) % LANES, 1), out)
        folded = fold(out, slices * cut)
        outs[k][0 : folded.shape[0]] = folded
        outs[k][folded.shape[0] :] = ground


def join_kernel(dims, *refs):
    slices, rows, group, cut = dims
    pieces, states, bed = refs[:group], refs[group], refs[group + 1]
    me = lax.axis_index("tm")
    height = rows * slices * cut // LANES
    for target, used, low, count in [(states.at[s], slices * cut, s * cut, height) for s in range(slices)] + [
        (bed, cut, 0, rows * cut // LANES)
    ]:
        base = 0 if count == height and target is not bed else height
        lane = lane_of((count, LANES))
        for i in range(LANES // used):
            out = jnp.zeros((count, LANES), jnp.float32)
            for k in range(group):
                first = source(me, k, group) * cut
                moved = pltpu.roll(pieces[k][base : base + count], (first - i * used - low + 2 * LANES) % LANES, 1)
                out = jnp.where((lane >= first) & (lane < first + cut), moved, out)
            target[i * count : (i + 1) * count] = out


def step(states, bed, background_state, ice_mask, flow_rate, obs_cell, obs_value):
    slices, rows, cols = states.shape
    group = lax.axis_size("tm")
    cut = cols // group
    width = cut + 2 * HALO
    full = rows + 2 * HALO
    lists = slices * obs_cell.shape[-1] // LANES
    f32 = lambda *shape: jax.ShapeDtypeStruct(shape, jnp.float32)
    vmem = lambda *shape: pltpu.VMEM(shape, jnp.float32)

    swaps_y = neighbour_swaps("gy")
    sides = len(swaps_y)
    own, *sends = call(
        functools.partial(copy_kernel, (slices, rows, cols, lists, sides)),
        [f32((slices + 4) * rows + 2 * lists, cols)] + [f32(rows + 2 * lists, LANES)] * sides,
        [pltpu.with_memory_space_constraint(v, pltpu.HBM) for v in (states, bed, background_state, ice_mask, flow_rate, obs_cell.reshape(lists, LANES), obs_value.reshape(lists, LANES))],
        [pltpu.VMEM((rows, cols), jnp.int32), pltpu.VMEM((lists, LANES), jnp.int32), pltpu.SemaphoreType.DMA((slices + 6,))],
        inputs=pltpu.HBM,
    )
    near = swap_all(sends, "gy")
    dims = (slices, rows, cols, lists, group, sides, cut, width)
    block = f32(rows + 2 * lists * (1 + sides), LANES)
    far = tuple(range(1, min(group, 2)))
    rest = (0, *range(2, group))
    first = []
    if far:
        first = call(functools.partial(pack_kernel, (*dims, far)), [block], [own, *near])
    *others, statics = call(
        functools.partial(pack_kernel, (*dims, rest)), [block] * len(rest) + [f32(2, rows, LANES)], [own, *near]
    )
    blocks = [others[0], *first, *others[1:]]
    blocks = exchange_all(blocks)
    maps = []
    for part in (blocks[:1], blocks[1:]):
        if part:
            maps += call(functools.partial(maps_kernel, dims), [f32(2, rows, LANES)] * len(part), part)
    early, late = [], []
    swaps = len(neighbour_swaps("gx"))
    stride = HALO + 2 * REACH
    if swaps:
        sends = call(
            functools.partial(edge_kernel, (rows, 1, swaps)),
            [f32(stride + 2 * HALO, LANES)] * swaps,
            [blocks[0], maps[0], statics],
        )
        early = swap_all(sends, "gx")
        late = early
        if group > 1:
            sends = call(
                functools.partial(edge_kernel, (rows, group - 1, swaps)),
                [f32((group - 1) * stride, LANES)] * swaps,
                [*blocks[1:], *maps[1:]],
            )
            late = swap_all(sends, "gx")
    packed = call(
        functools.partial(main_kernel, (slices, rows, group, swaps, cut, width)),
        [f32(rows * (slices + 1) * cut // LANES, LANES)] * group,
        [*blocks, statics, *maps, *early, *late],
        [vmem(group, full, LANES)] * 3
        + [vmem(3, full, LANES)]
        + [vmem(group, full, LANES)] * 2
        + [vmem(group, STEPS, 4, full, LANES), vmem(4, full, LANES), vmem(2, group, full + 16, LANES)],
    )
    pieces = exchange_all(packed)
    return tuple(
        call(
            functools.partial(join_kernel, (slices, rows, group, cut)),
            [f32(slices, rows, cols), f32(rows, cols)],
            pieces,
        )
    )


def solution(mesh):
    placed = (
        P("tm", "gx", "gy"),
        P("gx", "gy"),
        P("gx", "gy"),
        P("gx", "gy"),
        P("gx", "gy"),
        P("tm", "gx", "gy", None),
        P("tm", "gx", "gy", None),
    )
    return jax.shard_map(
        step,
        mesh=mesh,
        in_specs=placed,
        out_specs=(P("tm", "gx", "gy"), P("gx", "gy")),
        check_vma=False,
    )
```
